128 devices in a mesh: row: 8 (over y_hi, x), col: 16 (over z, y_lo, core).
Axes of the slice: x: 4, y: 4 (y_hi: 2, y_lo: 2; y = y_hi * 2 + y_lo), z: 4, core: 2. Of those that a mesh axis runs over, the one named last changes fastest.
Arguments:
- amps: float32 [4096, 9216], P('row', 'col'), may hold values from -6 to 6
- ladder_ints: float32 [4096, 4096], P('row', 'col'), may hold values from -0.25 to 0.25
- cycle_ints: float32 [6144, 6144], P(None, 'row'), may hold values from -0.21875 to 0.21875
- virt_irrep: int32 [64], replicated, may hold values from 0 to 7
- occ_irrep: int32 [96], replicated, may hold values from 0 to 7
- virt_energy: float32 [64], replicated, may hold values from 0.5 to 3
- occ_energy: float32 [96], replicated, may hold values from -3 to -0.5
Outputs:
- update: float32 [4096, 9216], P('row', 'col')
The draws below stay inside these ranges and needn't reach their ends.
All inputs are finite; a program needn't handle non-finite values.
Results may differ from the reference program's by a relative error of at most 0.00005.
Values sent between devices are 32-bit elements; how exact they have to be, the bound alone decides.
A program may use at most 128 MiB of HBM per device.

```python
import jax
import jax.numpy as jnp
from jax import lax

VS = 64
OS = 96
P_SIZE = 4096
IJ = 9216
Q = 6144


def with_ends(drawn, rng, low, high):
    dims = drawn.shape
    spot = [jax.random.randint(jax.random.fold_in(rng, axis), (), 0, dims[axis]) for axis in range(len(dims))]
    drawn = drawn.at[tuple(spot)].set(low)
    longest = dims.index(max(dims))
    spot[longest] = (spot[longest] + 1) % dims[longest]
    return drawn.at[tuple(spot)].set(high)


def steps_of(rng, dims, shards, least, top_value):
    gain = 1.0
    for dim, shards_of in shards:
        steps = jax.random.uniform(jax.random.fold_in(jax.random.fold_in(rng, 6), dim), (shards_of,), jnp.float32, least / len(shards), top_value / len(shards))
        gain = gain * jnp.repeat(jnp.exp(steps), dims[dim] // shards_of).reshape((-1,) + (1,) * (len(dims) - 1 - dim))
    return gain


def scatter_about(own_key, extent, deviation, reach, pieces=(), kind=jnp.bfloat16):
    drawn = jax.random.normal(own_key, extent, jnp.float32) * deviation
    if len(pieces) > 0:
        drawn = steps_of(own_key, extent, pieces, -0.22, 0.18) * drawn
    return jnp.clip(drawn, min=-reach, max=reach).astype(kind)


def setup_inputs(seed: int = 0) -> dict:
    streams_of = jax.random.split(jax.random.key(seed), 8)
    amps = scatter_about(streams_of[0], (P_SIZE, IJ), 1.0, 6.0, ((0, 8), (1, 16)), jnp.float32)
    ladder_ints = scatter_about(streams_of[1], (P_SIZE, P_SIZE), (VS * VS // 8) ** -0.5, 0.25, ((0, 8), (1, 16)), jnp.float32)
    cycle_ints = scatter_about(streams_of[2], (Q, Q), (VS * OS // 8) ** -0.5, 0.21875, ((1, 8),), jnp.float32)
    virt_irrep = with_ends(jax.random.randint(streams_of[3], (VS,), 0, 8), jax.random.fold_in(streams_of[3], 1), 0, 7).astype(jnp.int32)
    occ_irrep = with_ends(jax.random.randint(streams_of[4], (OS,), 0, 8), jax.random.fold_in(streams_of[4], 1), 0, 7).astype(jnp.int32)
    virt_energy = jnp.clip(jax.random.uniform(streams_of[5], (VS,), jnp.float32, 0.5, 3.0), 0.5, 3.0)
    occ_energy = jnp.clip(jax.random.uniform(streams_of[6], (OS,), jnp.float32, -3.0, -0.5), -3.0, -0.5)
    return dict(amps=amps, ladder_ints=ladder_ints, cycle_ints=cycle_ints, virt_irrep=virt_irrep, occ_irrep=occ_irrep, virt_energy=virt_energy, occ_energy=occ_energy)


def pair_labels(first, second):
    return jnp.bitwise_xor(first[:, None], second[None, :]).reshape(-1)


def reference(amps, ladder_ints, cycle_ints, virt_irrep, occ_irrep, virt_energy, occ_energy):
    highest = lax.Precision.HIGHEST
    virt_pairs = pair_labels(virt_irrep, virt_irrep)
    ladder_masked = jnp.where(virt_pairs[:, None] == virt_pairs[None, :], ladder_ints, jnp.float32(0.0))
    ladder = jnp.dot(ladder_masked, amps, precision=highest, preferred_element_type=jnp.float32)
    cycle_amps = amps.reshape(VS, VS, OS, OS).transpose(0, 2, 1, 3).reshape(VS * OS, VS * OS)
    mixed_pairs = pair_labels(virt_irrep, occ_irrep)
    cycle_masked = jnp.where(mixed_pairs[:, None] == mixed_pairs[None, :], cycle_ints, jnp.float32(0.0))
    cycle = jnp.dot(cycle_masked, cycle_amps, precision=highest, preferred_element_type=jnp.float32)
    cycle_back = cycle.reshape(VS, OS, VS, OS).transpose(0, 2, 1, 3).reshape(VS * VS, OS * OS)
    row_energy = (virt_energy[:, None] + virt_energy[None, :]).reshape(-1)
    col_energy = (occ_energy[:, None] + occ_energy[None, :]).reshape(-1)
    return (ladder + cycle_back) / (row_energy[:, None] - col_energy[None, :])
```

```python
import functools

import jax
import jax.numpy as jnp
import numpy as np
from jax import lax
from jax.experimental import pallas as pl
from jax.experimental.pallas import tpu as pltpu
from jax.sharding import PartitionSpec as P

MESH = pl.DeviceIdType.MESH
F32, BF16 = jnp.float32, jnp.bfloat16

VT, OT = 64, 96
VL, OL, VC = 8, 6, 4
CK = VL * OT
BJ = VC * OT
BLK = VL * OL
AB = VL * VT
CD = 256
HIJ = OL * OT // 2

A2A, BACK = 0, 16
YT, X1, X2, LY, LZ, LZ2, LC, OB = 32, 33, 35, 37, 40, 42, 44, 48
RS, YR = 49, 55
NSEM = 56


def split2(value):
    high = value.astype(BF16)
    low = (value - high.astype(F32)).astype(BF16)
    return high, low


def dot(a, b):
    return jnp.dot(a, b, preferred_element_type=F32)


def dot_nt(a, b):
    return lax.dot_general(a, b, (((1,), (1,)), ((), ())), preferred_element_type=F32)


def kernel(
    virt_ref, s_ref, tt_ref, l_ref, w_ref, ml_ref, vl_ref, oi_ref, vb_ref, p_ref, q_ref,
    lo_ref, d_ref,
    tx, lx, ca, ca_hi, ca_lo, wbuf, w_hi, w_lo, part, recv, yrecv, oacc, l_hi, l_lo, cp,
    ssem, rsem, wsem, lsem,
):
    row, col = lax.axis_index("row"), lax.axis_index("col")
    yh, x = row // 4, row % 4
    z, yl, core = col // 4, (col // 2) % 2, col % 2
    yme = yh * 2 + yl
    xp, xm, xo = (x + 1) % 4, (x + 3) % 4, (x + 2) % 4
    zp, zm, zo = (z + 1) % 4, (z + 3) % 4, (z + 2) % 4
    right, left = (yh * 4 + xp, col), (yh * 4 + xm, col)
    up, down = (row, zp * 4 + col % 4), (row, zm * 4 + col % 4)
    yrow = (1 - yh) * 4 + x
    ycol = z * 4 + (1 - yl) * 2 + core
    opp = (yrow, col)
    mate = (row, z * 4 + yl * 2 + (1 - core))

    def rc(src, dst, k, dev):
        return pltpu.make_async_remote_copy(
            src_ref=src, dst_ref=dst, send_sem=ssem.at[k], recv_sem=rsem.at[k],
            device_id=dev, device_id_type=MESH,
        )

    def rows48(ref, index):
        return ref.at[pl.ds(pl.multiple_of(index * BLK, BLK), BLK), :]

    bar = pltpu.get_barrier_semaphore()

    def greet(d, carry):
        pl.semaphore_signal(bar, inc=1, device_id=(row, col ^ d), device_id_type=MESH)
        return carry

    lax.fori_loop(1, 16, greet, 0)
    for dev in (right, left, up, down, opp, (yrow, ycol)):
        pl.semaphore_signal(bar, inc=1, device_id=dev, device_id_type=MESH)
    pl.semaphore_wait(bar, 21)

    def a2a_copy(d):
        return rc(rows48(s_ref, col ^ d), rows48(ca, col), A2A + d, (row, col ^ d))

    yt = rc(tt_ref.at[1 - yh], tx.at[x, yh], YT, opp)
    yt.start()
    lax.fori_loop(1, 16, lambda d, n: (a2a_copy(d).start(), n)[1], 0)
    own_t = pltpu.make_async_copy(tt_ref.at[yh], tx.at[x, yh], lsem.at[0])
    own_t.start()
    own_s = pltpu.make_async_copy(rows48(s_ref, col), rows48(ca, col), lsem.at[1])
    own_s.start()
    own_l = pltpu.make_async_copy(l_ref, lx.at[core, z, yme], lsem.at[2])
    own_l.start()
    ydevs = [(row, ycol), (yrow, ycol), opp]
    ly = [rc(l_ref, lx.at[core, z, yme], LY + n, dev) for n, dev in enumerate(ydevs)]
    for copy in ly:
        copy.start()

    order = [(xo, 1 - yh), (xo, yh), (xm, 1 - yh), (xp, 1 - yh), (xp, yh), (xm, yh), (x, 1 - yh), (x, yh)]

    def w_copy(t):
        dx, dy = order[t]
        return pltpu.make_async_copy(w_ref.at[dy * 4 + dx], wbuf.at[t % 2], wsem.at[t % 2])

    w_copy(0).start()
    w_copy(1).start()

    def w_split(t):
        dx, dy = order[t]
        own = ml_ref[row]

        def step(a, carry):
            rows = pl.ds(pl.multiple_of(a * OT, OT), OT)
            labels = oi_ref[...] ^ virt_ref[(dy * 4 + dx) * VL + a]
            kept = jnp.where(labels == own, wbuf[t % 2, rows, :], 0.0)
            high, low = split2(kept)
            w_hi[rows, :] = high
            w_lo[rows, :] = low
            return carry

        lax.fori_loop(0, VL, step, 0)

    def w_mm(t):
        def step(n, carry):
            rows = pl.ds(pl.multiple_of(n * 256, 256), 256)
            high, low = w_hi[rows, :], w_lo[rows, :]
            part[t, rows, :] = dot(high, ca_hi[...]) + dot(high, ca_lo[...]) + dot(low, ca_hi[...])
            return carry

        lax.fori_loop(0, CK // 256, step, 0)

    def cyc(t):
        if t > 0:
            w_copy(t).wait()
            w_split(t)
            if t + 2 < 8:
                w_copy(t + 2).start()
        w_mm(t)

    def add_into(dst, src):
        def step(n, carry):
            rows = pl.ds(pl.multiple_of(n * 96, 96), 96)
            dst[rows, :] = dst[rows, :] + src[rows, :]
            return carry

        lax.fori_loop(0, CK // 96, step, 0)

    w_copy(0).wait()
    w_split(0)
    w_copy(2).start()

    own_t.wait()
    yt.wait_send()
    pltpu.make_async_remote_copy(
        src_ref=tt_ref.at[1 - yh], dst_ref=tx.at[x, 1 - yh], send_sem=ssem.at[YT], recv_sem=rsem.at[YT],
        device_id=opp, device_id_type=MESH,
    ).wait_recv()
    x1 = [rc(tx.at[x], tx.at[x], X1 + n, dev) for n, dev in enumerate((right, left))]
    for copy in x1:
        copy.start()

    own_s.wait()

    def a2a_wait(d, carry):
        a2a_copy(d).wait_send()
        rc(rows48(s_ref, col), rows48(ca, col ^ d), A2A + d, (row, col ^ d)).wait_recv()
        return carry

    lax.fori_loop(1, 16, a2a_wait, 0)

    def ca_step(n, carry):
        rows = pl.ds(pl.multiple_of(n * 256, 256), 256)
        high, low = split2(ca[...])
        ca_hi[rows, :] = dot(p_ref[rows, :], high).astype(BF16)
        ca_lo[rows, :] = dot(p_ref[rows, :], low).astype(BF16)
        return carry

    lax.fori_loop(0, CK // 256, ca_step, 0)

    rs = [
        rc(part.at[0], recv.at[0], RS + 0, right),
        rc(part.at[1], recv.at[1], RS + 1, left),
        rc(part.at[2], recv.at[2], RS + 2, left),
        rc(part.at[3], recv.at[3], RS + 3, right),
        rc(part.at[4], recv.at[4], RS + 4, right),
        rc(part.at[5], recv.at[5], RS + 5, left),
    ]
    cyc(0)
    rs[0].start()
    cyc(1)
    rs[1].start()

    own_l.wait()
    lyw = []
    for n, (dst_y) in enumerate((yh * 2 + 1 - yl, (1 - yh) * 2 + 1 - yl, (1 - yh) * 2 + yl)):
        ly[n].wait_send()
        rc(l_ref, lx.at[core, z, dst_y], LY + n, ydevs[n]).wait_recv()
    lz = [rc(lx.at[core, z], lx.at[core, z], LZ + n, dev) for n, dev in enumerate((up, down))]
    for copy in lz:
        copy.start()
    lc = [rc(lx.at[core, zz], lx.at[core, zz], LC + n, mate) for n, zz in enumerate((z, zm, zp, zo))]
    lc[0].start()

    cyc(2)
    rs[2].start()
    cyc(3)
    rs[0].wait_recv()
    add_into(part.at[3], recv.at[0])
    rs[3].start()
    cyc(4)
    rs[4].start()
    cyc(5)
    rs[1].wait_recv()
    add_into(part.at[5], recv.at[1])
    rs[5].start()

    rc(tx.at[xm], tx.at[xm], X1 + 0, left).wait_recv()
    rc(tx.at[xp], tx.at[xp], X1 + 1, right).wait_recv()
    x2 = [
        rc(tx.at[xm, 0], tx.at[xm, 0], X2 + 0, right),
        rc(tx.at[xp, 1], tx.at[xp, 1], X2 + 1, left),
    ]
    for copy in x2:
        copy.start()
    rc(lx.at[core, zm], lx.at[core, zm], LZ + 0, down).wait_recv()
    rc(lx.at[core, zp], lx.at[core, zp], LZ + 1, up).wait_recv()
    lz2 = [
        rc(lx.at[core, zm, pl.ds(0, 2)], lx.at[core, zm, pl.ds(0, 2)], LZ2 + 0, up),
        rc(lx.at[core, zp, pl.ds(2, 2)], lx.at[core, zp, pl.ds(2, 2)], LZ2 + 1, down),
    ]
    for copy in lz2:
        copy.start()
    lc[1].start()
    lc[2].start()

    cyc(6)
    cyc(7)

    rc(lx.at[core, zo, pl.ds(0, 2)], lx.at[core, zo, pl.ds(0, 2)], LZ2 + 0, down).wait_recv()
    rc(lx.at[core, zo, pl.ds(2, 2)], lx.at[core, zo, pl.ds(2, 2)], LZ2 + 1, up).wait_recv()
    lc[3].start()

    rs[3].wait_recv()
    rs[2].wait_recv()
    add_into(part.at[6], recv.at[3])
    add_into(part.at[6], recv.at[2])
    yr = rc(part.at[6], yrecv, YR, opp)
    yr.start()

    rc(tx.at[xo, 0], tx.at[xo, 0], X2 + 0, left).wait_recv()
    rc(tx.at[xo, 1], tx.at[xo, 1], X2 + 1, right).wait_recv()
    for n, zz in enumerate((z, zm, zp, zo)):
        rc(lx.at[1 - core, zz], lx.at[1 - core, zz], LC + n, mate).wait_recv()

    for h in range(2):
        oacc[h] = jnp.zeros((HIJ, AB), F32)

    def ladder(n, carry):
        kc, zz, yy = n // 16, (n // 4) % 4, n % 4
        cc = zz * 4 + (yy % 2) * 2 + kc
        h = yy // 2
        source = cc // 2

        def mask_step(a, inner):
            rows = pl.ds(pl.multiple_of(a * VT, VT), VT)
            labels = vb_ref[...] ^ virt_ref[(h * 4 + x) * VL + a]
            kept = jnp.where(labels == vl_ref[cc], lx[kc, zz, yy, rows, :], 0.0)
            high, low = split2(kept)
            l_hi[rows, :] = high
            l_lo[rows, :] = low
            return inner

        lax.fori_loop(0, VL, mask_step, 0)
        lanes = pl.ds(pl.multiple_of(kc * CD, CD), CD)
        t_hi, t_lo = split2(tx[source % 4, source // 4, :, lanes])
        oacc[h] = oacc[h] + (dot_nt(t_hi, l_hi[...]) + dot_nt(t_lo, l_hi[...]) + dot_nt(t_hi, l_lo[...]))
        return carry

    lax.fori_loop(0, 32, ladder, 0)
    out_own = pltpu.make_async_copy(oacc.at[yh], lo_ref.at[yh], lsem.at[0])
    out_own.start()
    ob = rc(oacc.at[1 - yh], lo_ref.at[yh], OB, opp)
    ob.start()

    rs[4].wait_recv()
    rs[5].wait_recv()
    add_into(part.at[7], recv.at[4])
    add_into(part.at[7], recv.at[5])
    yr.wait_recv()
    add_into(part.at[7], yrecv)

    def back_step(n, carry):
        rows = pl.ds(pl.multiple_of(n * 256, 256), 256)
        value = part[7]
        high, low = split2(value)
        rest = (value - high.astype(F32) - low.astype(F32)).astype(BF16)
        sel = q_ref[rows, :]
        cp[rows, :] = dot(sel, high) + dot(sel, low) + dot(sel, rest)
        return carry

    lax.fori_loop(0, CK // 256, back_step, 0)

    def back_copy(d):
        return rc(rows48(cp, col ^ d), rows48(d_ref, col), BACK + d, (row, col ^ d))

    lax.fori_loop(1, 16, lambda d, n: (back_copy(d).start(), n)[1], 0)
    own_d = pltpu.make_async_copy(rows48(cp, col), rows48(d_ref, col), lsem.at[1])
    own_d.start()

    for copy in x1 + x2 + lz + lz2 + lc + rs + [yr, ob]:
        copy.wait_send()
    rc(oacc.at[yh], lo_ref.at[1 - yh], OB, opp).wait_recv()
    out_own.wait()
    own_d.wait()

    def back_wait(d, carry):
        back_copy(d).wait_send()
        rc(rows48(cp, col), rows48(d_ref, col ^ d), BACK + d, (row, col ^ d)).wait_recv()
        return carry

    lax.fori_loop(1, 16, back_wait, 0)


def permutation():
    a, c, i = np.meshgrid(np.arange(VL), np.arange(16), np.arange(OL), indexing="ij")
    table = np.zeros((CK, CK), np.float32)
    table[(a * OT + c * OL + i).reshape(-1), (c * BLK + a * OL + i).reshape(-1)] = 1.0
    return table


def body(amps, ladder_ints, cycle_ints, virt_irrep, occ_irrep, virt_energy, occ_energy):
    row, col = lax.axis_index("row"), lax.axis_index("col")
    sent = amps.reshape(VL, 16, VC, OL, OT).transpose(1, 0, 3, 2, 4).reshape(CK, BJ)
    turned = amps.T.reshape(2, HIJ, AB)
    mixed = (virt_irrep[:, None] ^ occ_irrep[None, :]).reshape(8, 1, CK)
    pairs = (virt_irrep[:, None] ^ virt_irrep[None, :]).reshape(16, 1, CD)
    table = permutation()
    forward = jnp.asarray(table, BF16)
    backward = jnp.asarray(table.T, BF16)
    anywhere = pl.BlockSpec(memory_space=pl.ANY)
    vmem = pl.BlockSpec(memory_space=pltpu.VMEM)
    ladder, cycle = pl.pallas_call(
        kernel,
        out_shape=(
            jax.ShapeDtypeStruct((2, HIJ, AB), F32),
            jax.ShapeDtypeStruct((CK, BJ), F32),
        ),
        in_specs=[pl.BlockSpec(memory_space=pltpu.SMEM)] + [anywhere] * 4 + [vmem] * 6,
        out_specs=(anywhere, anywhere),
        scratch_shapes=[
            pltpu.VMEM((4, 2, HIJ, AB), F32),
            pltpu.VMEM((2, 4, 4, AB, CD), F32),
            pltpu.VMEM((CK, BJ), F32),
            pltpu.VMEM((CK, BJ), BF16),
            pltpu.VMEM((CK, BJ), BF16),
            pltpu.VMEM((2, CK, CK), F32),
            pltpu.VMEM((CK, CK), BF16),
            pltpu.VMEM((CK, CK), BF16),
            pltpu.VMEM((8, CK, BJ), F32),
            pltpu.VMEM((6, CK, BJ), F32),
            pltpu.VMEM((CK, BJ), F32),
            pltpu.VMEM((2, HIJ, AB), F32),
            pltpu.VMEM((AB, CD), BF16),
            pltpu.VMEM((AB, CD), BF16),
            pltpu.VMEM((CK, BJ), F32),
            pltpu.SemaphoreType.DMA((NSEM,)),
            pltpu.SemaphoreType.DMA((NSEM,)),
            pltpu.SemaphoreType.DMA((2,)),
            pltpu.SemaphoreType.DMA((3,)),
        ],
        compiler_params=pltpu.CompilerParams(
            collective_id=0, has_side_effects=True, vmem_limit_bytes=67043328
        ),
    )(
        virt_irrep, sent, turned, ladder_ints, cycle_ints.reshape(8, CK, CK), mixed, pairs,
        occ_irrep.reshape(OT, 1), virt_irrep.reshape(VT, 1), forward, backward,
    )
    back = cycle.reshape(16, VL, OL, VC, OT).transpose(1, 0, 3, 2, 4).reshape(AB, OL * OT)
    own_virt = lax.dynamic_slice_in_dim(virt_energy, row * VL, VL)
    own_occ = lax.dynamic_slice_in_dim(occ_energy, col * OL, OL)
    row_energy = (own_virt[:, None] + virt_energy[None, :]).reshape(-1)
    col_energy = (own_occ[:, None] + occ_energy[None, :]).reshape(-1)
    return (ladder.reshape(OL * OT, AB).T + back) / (row_energy[:, None] - col_energy[None, :])


def solution(mesh):
    placed = (P("row", "col"), P("row", "col"), P(None, "row"), P(), P(), P(), P())
    return jax.shard_map(
        body, mesh=mesh, in_specs=placed, out_specs=P("row", "col"), check_vma=False
    )
```

```python
import functools

import jax
import jax.numpy as jnp
import numpy as np
from jax import lax
from jax.experimental import pallas as pl
from jax.experimental.pallas import tpu as pltpu
from jax.sharding import PartitionSpec as P

MESH = pl.DeviceIdType.MESH
F32, BF16 = jnp.float32, jnp.bfloat16

VT, OT = 64, 96
VL, OL, VC = 8, 6, 4
CK = VL * OT
BJ = VC * OT
HALF = CK // 2
BLK = VL * OL // 2
AB = VL * VT
CD = 256
HIJ = OL * OT // 2

A2A, BACK = 0, 16
YT, X1, X2, LY, LZ, LZ2, LC, OB = 32, 33, 37, 39, 42, 50, 52, 56
RS, YR, BACK2 = 57, 65, 66
NSEM = 83


def split2(value):
    high = value.astype(BF16)
    low = (value - high.astype(F32)).astype(BF16)
    return high, low


def dot(a, b):
    return jnp.dot(a, b, preferred_element_type=F32)


def kernel(
    virt_ref, s_ref, tt_ref, l_ref, w_ref, virt_lanes, occ_lanes, p_ref, q_ref,
    lo_ref, d_ref,
    tx, lx, ca, ca_hi, ca_lo, wbuf, w_hi, w_lo, part, recv, yrecv, oacc, lmask, cp, ml_ref, vl_ref, oi_ref, vb_ref,
    ssem, rsem, wsem, lsem,
):
    row, col = lax.axis_index("row"), lax.axis_index("col")
    yh, x = row // 4, row % 4
    z, yl, core = col // 4, (col // 2) % 2, col % 2
    yme = yh * 2 + yl
    xp, xm, xo = (x + 1) % 4, (x + 3) % 4, (x + 2) % 4
    zp, zm, zo = (z + 1) % 4, (z + 3) % 4, (z + 2) % 4
    right, left = (yh * 4 + xp, col), (yh * 4 + xm, col)
    up, down = (row, zp * 4 + col % 4), (row, zm * 4 + col % 4)
    yrow = (1 - yh) * 4 + x
    ycol = z * 4 + (1 - yl) * 2 + core
    opp = (yrow, col)
    mate = (row, z * 4 + yl * 2 + (1 - core))

    def rc(src, dst, k, dev):
        return pltpu.make_async_remote_copy(
            src_ref=src, dst_ref=dst, send_sem=ssem.at[k], recv_sem=rsem.at[k],
            device_id=dev, device_id_type=MESH,
        )

    def upright(lanes, count):
        spread = jnp.broadcast_to(lanes, (count, count))
        at = lax.broadcasted_iota(jnp.int32, (count, count), 0) == lax.broadcasted_iota(jnp.int32, (count, count), 1)
        return jnp.sum(jnp.where(at, spread, 0), axis=1, keepdims=True)

    oi_ref[...] = upright(occ_lanes[...], OT)
    vb_ref[...] = upright(virt_lanes[...], VT)
    for a in range(VL):
        ml_ref[:, a * OT : (a + 1) * OT] = occ_lanes[...] ^ virt_ref[row * VL + a]
    for a in range(VC):
        vl_ref[:, a * VT : (a + 1) * VT] = virt_lanes[...] ^ virt_ref[col * VC + a]

    def l_step(a, carry):
        rows = pl.ds(pl.multiple_of(a * VT, VT), VT)
        labels = vb_ref[...] ^ virt_ref[row * VL + a]
        lmask[rows, :] = jnp.where(labels == vl_ref[...], l_ref[rows, :], 0.0)
        return carry

    lax.fori_loop(0, VL, l_step, 0)
    lx[core, z, yme] = lmask[...].T

    bar = pltpu.get_barrier_semaphore()

    def greet(d, carry):
        pl.semaphore_signal(bar, inc=1, device_id=(row, col ^ d), device_id_type=MESH)
        return carry

    lax.fori_loop(1, 16, greet, 0)
    for dev in (right, left, up, down, opp, (yrow, ycol)):
        pl.semaphore_signal(bar, inc=1, device_id=dev, device_id_type=MESH)
    pl.semaphore_wait(bar, 21)

    def a2a_copy(d):
        return rc(s_ref.at[:, col ^ d], ca.at[:, col], A2A + d, (row, col ^ d))

    yt = rc(tt_ref.at[1 - yh], tx.at[x, yh], YT, opp)
    yt.start()
    x1 = [rc(tt_ref.at[yh], tx.at[x, yh], X1 + n, dev) for n, dev in enumerate((right, left))]
    for copy in x1:
        copy.start()
    lax.fori_loop(1, 16, lambda d, n: (a2a_copy(d).start(), n)[1], 0)
    own_t = pltpu.make_async_copy(tt_ref.at[yh], tx.at[x, yh], lsem.at[0])
    own_t.start()
    own_s = pltpu.make_async_copy(s_ref.at[:, col], ca.at[:, col], lsem.at[1])
    own_s.start()
    own_l = lx.at[core, z, yme]
    ydevs = [(row, ycol), (yrow, ycol), opp]
    yidx = [yh * 2 + 1 - yl, (1 - yh) * 2 + 1 - yl, (1 - yh) * 2 + yl]
    ly = [rc(own_l, own_l, LY + n, dev) for n, dev in enumerate(ydevs)]
    for copy in ly:
        copy.start()
    lz = [rc(own_l, own_l, LZ + n, dev) for n, dev in enumerate((up, down))]
    for copy in lz:
        copy.start()

    order = [(xo, 1 - yh), (xo, yh), (xm, 1 - yh), (xp, 1 - yh), (xp, yh), (xm, yh), (x, 1 - yh), (x, yh)]

    def w_copy(t):
        dx, dy = order[t]
        return pltpu.make_async_copy(w_ref.at[dy * 4 + dx], wbuf.at[t % 2], wsem.at[t % 2])

    w_copy(0).start()
    w_copy(1).start()

    def w_split(t):
        dx, dy = order[t]
        own = ml_ref[...]

        def step(a, carry):
            rows = pl.ds(pl.multiple_of(a * OT, OT), OT)
            labels = oi_ref[...] ^ virt_ref[(dy * 4 + dx) * VL + a]
            kept = jnp.where(labels == own, wbuf[t % 2, rows, :], 0.0)
            high, low = split2(kept)
            w_hi[rows, :] = high
            w_lo[rows, :] = low
            return carry

        lax.fori_loop(0, VL, step, 0)

    def w_mm(t):
        def step(n, carry):
            rows = pl.ds(pl.multiple_of(n * 256, 256), 256)
            high, low = w_hi[rows, :], w_lo[rows, :]
            part[t, rows, :] = dot(high, ca_hi[...]) + dot(high, ca_lo[...]) + dot(low, ca_hi[...])
            return carry

        lax.fori_loop(0, CK // 256, step, 0)

    def cyc(t):
        if t > 0:
            w_copy(t).wait()
            w_split(t)
            if t + 2 < 8:
                w_copy(t + 2).start()
        w_mm(t)

    def add_into(dst, src):
        def step(n, carry):
            rows = pl.ds(pl.multiple_of(n * 96, 96), 96)
            dst[rows, :] = dst[rows, :] + src[rows, :]
            return carry

        lax.fori_loop(0, CK // 96, step, 0)

    w_copy(0).wait()
    w_split(0)
    w_copy(2).start()

    own_t.wait()
    yt.wait_send()
    pltpu.make_async_remote_copy(
        src_ref=tt_ref.at[1 - yh], dst_ref=tx.at[x, 1 - yh], send_sem=ssem.at[YT], recv_sem=rsem.at[YT],
        device_id=opp, device_id_type=MESH,
    ).wait_recv()
    x1b = [rc(tx.at[x, 1 - yh], tx.at[x, 1 - yh], X1 + 2 + n, dev) for n, dev in enumerate((right, left))]
    for copy in x1b:
        copy.start()

    own_s.wait()

    def a2a_wait(d, carry):
        a2a_copy(d).wait_send()
        rc(s_ref.at[:, col], ca.at[:, col ^ d], A2A + d, (row, col ^ d)).wait_recv()
        return carry

    lax.fori_loop(1, 16, a2a_wait, 0)

    for half in range(2):
        high, low = split2(ca[half].reshape(HALF, BJ))
        rows = pl.ds(half * HALF, HALF)
        ca_hi[rows, :] = dot(p_ref[...], high).astype(BF16)
        ca_lo[rows, :] = dot(p_ref[...], low).astype(BF16)

    rs = [
        rc(part.at[0], recv.at[0], RS + 0, right),
        rc(part.at[1], recv.at[1], RS + 1, left),
        rc(part.at[2], recv.at[2], RS + 2, left),
        rc(part.at[3], recv.at[3], RS + 3, right),
    ]
    halves = [pl.ds(0, HALF), pl.ds(HALF, HALF)]
    rs4 = [rc(part.at[4, rows], recv.at[4, rows], RS + 4 + n, right) for n, rows in enumerate(halves)]
    rs5 = [rc(part.at[5, rows], recv.at[5, rows], RS + 6 + n, left) for n, rows in enumerate(halves)]
    cyc(0)
    rs[0].start()
    cyc(1)
    rs[1].start()

    for n, dst_y in enumerate(yidx):
        ly[n].wait_send()
        block = lx.at[core, z, dst_y]
        rc(own_l, block, LY + n, ydevs[n]).wait_recv()
        for m, dev in enumerate((up, down)):
            copy = rc(block, block, LZ + 2 + 2 * n + m, dev)
            copy.start()
            lz.append(copy)
    lc = [rc(lx.at[core, zz], lx.at[core, zz], LC + n, mate) for n, zz in enumerate((z, zm, zp, zo))]
    lc[0].start()

    cyc(2)
    rs[2].start()
    cyc(3)
    rs[0].wait_recv()
    add_into(part.at[3], recv.at[0])
    rs[3].start()
    cyc(4)
    rs4[0].start()
    rs4[1].start()
    cyc(5)
    rs[1].wait_recv()
    add_into(part.at[5], recv.at[1])
    rs5[0].start()
    rs5[1].start()

    for h, base in ((yh, X1), (1 - yh, X1 + 2)):
        rc(tx.at[xm, h], tx.at[xm, h], base, left).wait_recv()
        rc(tx.at[xp, h], tx.at[xp, h], base + 1, right).wait_recv()
    x2 = [
        rc(tx.at[xm, 0], tx.at[xm, 0], X2 + 0, right),
        rc(tx.at[xp, 1], tx.at[xp, 1], X2 + 1, left),
    ]
    for copy in x2:
        copy.start()
    for n, src_y in enumerate([yme] + yidx):
        rc(lx.at[core, zm, src_y], lx.at[core, zm, src_y], LZ + 2 * n, down).wait_recv()
        rc(lx.at[core, zp, src_y], lx.at[core, zp, src_y], LZ + 2 * n + 1, up).wait_recv()
    lz2 = [
        rc(lx.at[core, zm, pl.ds(0, 2)], lx.at[core, zm, pl.ds(0, 2)], LZ2 + 0, up),
        rc(lx.at[core, zp, pl.ds(2, 2)], lx.at[core, zp, pl.ds(2, 2)], LZ2 + 1, down),
    ]
    for copy in lz2:
        copy.start()
    lc[1].start()
    lc[2].start()

    cyc(6)
    cyc(7)

    rs[3].wait_recv()
    rs[2].wait_recv()
    add_into(part.at[6], recv.at[3])
    add_into(part.at[6], recv.at[2])
    yr = [rc(part.at[6, rows], yrecv.at[rows], YR + 17 * n, opp) for n, rows in enumerate(halves)]
    for copy in yr:
        copy.start()

    rc(lx.at[core, zo, pl.ds(0, 2)], lx.at[core, zo, pl.ds(0, 2)], LZ2 + 0, down).wait_recv()
    rc(lx.at[core, zo, pl.ds(2, 2)], lx.at[core, zo, pl.ds(2, 2)], LZ2 + 1, up).wait_recv()
    lc[3].start()
    for n, zz in enumerate((z, zm, zp, zo)):
        rc(lx.at[1 - core, zz], lx.at[1 - core, zz], LC + n, mate).wait_recv()

    for h in range(2):
        oacc[h] = jnp.zeros((HIJ, AB), F32)

    def ladder(sx, n):
        kc, sy = n // 2, n % 2
        source = sy * 4 + sx
        zz, ylo = source // 2, source % 2
        lanes = pl.ds(pl.multiple_of(kc * CD, CD), CD)
        t_hi, t_lo = split2(tx[sx, sy, :, lanes])
        both = jnp.concatenate([t_hi, t_lo], axis=0)
        for h in range(2):
            high, low = split2(lx[kc, zz, h * 2 + ylo])
            wide = dot(both, high)
            oacc[h] = oacc[h] + (wide[:HIJ] + wide[HIJ:] + dot(t_hi, low))

    lax.fori_loop(0, 12, lambda n, carry: (ladder((x + 3 + n // 4) % 4, n % 4), carry)[1], 0)

    def back_copy(n, base, d):
        return rc(cp.at[n, col ^ d], d_ref.at[n, col], base + d, (row, col ^ d))

    own_d = [pltpu.make_async_copy(cp.at[n, col], d_ref.at[n, col], lsem.at[1 + n]) for n in range(2)]
    for n, base in ((0, BACK), (1, BACK2)):
        rows = halves[n]
        rs4[n].wait_recv()
        rs5[n].wait_recv()
        rc(part.at[6, rows], yrecv.at[rows], YR + 17 * n, opp).wait_recv()
        value = (part[7, rows, :] + recv[4, rows, :]) + (recv[5, rows, :] + yrecv[rows, :])
        high, low = split2(value)
        rest = (value - high.astype(F32) - low.astype(F32)).astype(BF16)
        sel = q_ref[...]
        cp[n] = (dot(sel, high) + dot(sel, low) + dot(sel, rest)).reshape(16, BLK, BJ)
        lax.fori_loop(1, 16, lambda d, carry: (back_copy(n, base, d).start(), carry)[1], 0)
        own_d[n].start()

    rc(tx.at[xo, 0], tx.at[xo, 0], X2 + 0, left).wait_recv()
    rc(tx.at[xo, 1], tx.at[xo, 1], X2 + 1, right).wait_recv()
    lax.fori_loop(0, 4, lambda n, carry: (ladder(xo, n), carry)[1], 0)
    out_own = pltpu.make_async_copy(oacc.at[yh], lo_ref.at[yh], lsem.at[0])
    out_own.start()
    ob = rc(oacc.at[1 - yh], lo_ref.at[yh], OB, opp)
    ob.start()

    for copy in x1 + x1b + x2 + lz + lz2 + lc + rs + rs4 + rs5 + yr + [ob]:
        copy.wait_send()
    rc(oacc.at[yh], lo_ref.at[1 - yh], OB, opp).wait_recv()
    out_own.wait()
    for n, base in ((0, BACK), (1, BACK2)):
        own_d[n].wait()

        def back_wait(d, carry):
            back_copy(n, base, d).wait_send()
            rc(cp.at[n, col], d_ref.at[n, col ^ d], base + d, (row, col ^ d)).wait_recv()
            return carry

        lax.fori_loop(1, 16, back_wait, 0)


def permutation():
    a, c, i = np.meshgrid(np.arange(VL // 2), np.arange(16), np.arange(OL), indexing="ij")
    table = np.zeros((HALF, HALF), np.float32)
    table[(a * OT + c * OL + i).reshape(-1), (c * BLK + a * OL + i).reshape(-1)] = 1.0
    return table


def body(amps, ladder_ints, cycle_ints, virt_irrep, occ_irrep, virt_energy, occ_energy):
    row, col = lax.axis_index("row"), lax.axis_index("col")
    sent = amps.reshape(2, VL // 2, 16, VC, OL, OT).transpose(0, 2, 1, 4, 3, 5).reshape(2, 16, BLK, BJ)
    turned = amps.T.reshape(2, HIJ, AB)
    table = permutation()
    forward = jnp.asarray(table, BF16)
    backward = jnp.asarray(table.T, BF16)
    anywhere = pl.BlockSpec(memory_space=pl.ANY)
    vmem = pl.BlockSpec(memory_space=pltpu.VMEM)
    ladder, cycle = pl.pallas_call(
        kernel,
        out_shape=(
            jax.ShapeDtypeStruct((2, HIJ, AB), F32),
            jax.ShapeDtypeStruct((2, 16, BLK, BJ), F32),
        ),
        in_specs=[pl.BlockSpec(memory_space=pltpu.SMEM)] + [anywhere] * 2 + [vmem, anywhere] + [vmem] * 4,
        out_specs=(anywhere, anywhere),
        scratch_shapes=[
            pltpu.VMEM((4, 2, HIJ, AB), F32),
            pltpu.VMEM((2, 4, 4, CD, AB), F32),
            pltpu.VMEM((2, 16, BLK, BJ), F32),
            pltpu.VMEM((CK, BJ), BF16),
            pltpu.VMEM((CK, BJ), BF16),
            pltpu.VMEM((2, CK, CK), F32),
            pltpu.VMEM((CK, CK), BF16),
            pltpu.VMEM((CK, CK), BF16),
            pltpu.VMEM((8, CK, BJ), F32),
            pltpu.VMEM((6, CK, BJ), F32),
            pltpu.VMEM((CK, BJ), F32),
            pltpu.VMEM((2, HIJ, AB), F32),
            pltpu.VMEM((AB, CD), F32),
            pltpu.VMEM((2, 16, BLK, BJ), F32),
            pltpu.VMEM((1, CK), jnp.int32),
            pltpu.VMEM((1, CD), jnp.int32),
            pltpu.VMEM((OT, 1), jnp.int32),
            pltpu.VMEM((VT, 1), jnp.int32),
            pltpu.SemaphoreType.DMA((NSEM,)),
            pltpu.SemaphoreType.DMA((NSEM,)),
            pltpu.SemaphoreType.DMA((2,)),
            pltpu.SemaphoreType.DMA((3,)),
        ],
        compiler_params=pltpu.CompilerParams(
            collective_id=0, has_side_effects=True, vmem_limit_bytes=67043328
        ),
    )(
        virt_irrep, sent, turned, ladder_ints, cycle_ints.reshape(8, CK, CK),
        virt_irrep.reshape(1, VT), occ_irrep.reshape(1, OT), forward, backward,
    )
    back = cycle.reshape(2, 16, VL // 2, OL, VC, OT).transpose(3, 5, 0, 2, 1, 4).reshape(OL * OT, AB)
    own_virt = lax.dynamic_slice_in_dim(virt_energy, row * VL, VL)
    own_occ = lax.dynamic_slice_in_dim(occ_energy, col * OL, OL)
    row_energy = (own_virt[:, None] + virt_energy[None, :]).reshape(-1)
    col_energy = (own_occ[:, None] + occ_energy[None, :]).reshape(-1)
    return ((ladder.reshape(OL * OT, AB) + back) / (row_energy[None, :] - col_energy[:, None])).T


def solution(mesh):
    placed = (P("row", "col"), P("row", "col"), P(None, "row"), P(), P(), P(), P())
    return jax.shard_map(
        body, mesh=mesh, in_specs=placed, out_specs=P("row", "col"), check_vma=False
    )
```

```python
import functools

import jax
import jax.numpy as jnp
import numpy as np
from jax import lax
from jax.experimental import pallas as pl
from jax.experimental.pallas import tpu as pltpu
from jax.sharding import PartitionSpec as P

MESH = pl.DeviceIdType.MESH
F32, BF16 = jnp.float32, jnp.bfloat16

VT, OT = 64, 96
VL, OL, VC = 8, 6, 4
CK = VL * OT
BJ = VC * OT
BLK = VL * OL
THIRD = BJ // 3
AB = VL * VT
CD = 256
HIJ = OL * OT // 2

A2A, BACK, YT, X1, X2, LY = 0, 16, 64, 65, 69, 73
LZ, LZ2, LC, OB, RS, YR = 76, 84, 86, 90, 91, 105
NSEM = 108


def split2(value):
    high = value.astype(BF16)
    low = (value - high.astype(F32)).astype(BF16)
    return high, low


def dot_nt(a, b):
    return lax.dot_general(a, b, (((1,), (1,)), ((), ())), preferred_element_type=F32)


def dot(a, b):
    return jnp.dot(a, b, preferred_element_type=F32)


def kernel(
    virt_ref, ve_ref, oe_ref, tt_ref, l_ref, w_ref, virt_lanes, occ_lanes, ve_lanes, oe_lanes, p_ref, q_ref,
    lo_ref, d_ref, row_e, col_e,
    tt, s_ref, tx, lx, raw, ca, ca_hi, ca_lo, wbuf, w_hi, w_lo, part, recv, yrecv, oacc, lmask, cp, ml_ref, vl_ref, oi_ref, vb_ref,
    ssem, rsem, wsem, lsem,
):
    row, col = lax.axis_index("row"), lax.axis_index("col")
    yh, x = row // 4, row % 4
    z, yl, core = col // 4, (col // 2) % 2, col % 2
    yme = yh * 2 + yl
    xp, xm, xo = (x + 1) % 4, (x + 3) % 4, (x + 2) % 4
    zp, zm, zo = (z + 1) % 4, (z + 3) % 4, (z + 2) % 4
    right, left = (yh * 4 + xp, col), (yh * 4 + xm, col)
    up, down = (row, zp * 4 + col % 4), (row, zm * 4 + col % 4)
    yrow = (1 - yh) * 4 + x
    ycol = z * 4 + (1 - yl) * 2 + core
    opp = (yrow, col)
    mate = (row, z * 4 + yl * 2 + (1 - core))

    def rc(src, dst, k, dev):
        return pltpu.make_async_remote_copy(
            src_ref=src, dst_ref=dst, send_sem=ssem.at[k], recv_sem=rsem.at[k],
            device_id=dev, device_id_type=MESH,
        )

    bar = pltpu.get_barrier_semaphore()

    def greet(d, carry):
        pl.semaphore_signal(bar, inc=1, device_id=(row, col ^ d), device_id_type=MESH)
        return carry

    lax.fori_loop(1, 16, greet, 0)
    for dev in (right, left, up, down, opp, (yrow, ycol)):
        pl.semaphore_signal(bar, inc=1, device_id=dev, device_id_type=MESH)

    load_t = pltpu.make_async_copy(tt_ref, tt, lsem.at[0])
    load_t.start()

    def upright(lanes, count):
        spread = jnp.broadcast_to(lanes, (count, count))
        at = lax.broadcasted_iota(jnp.int32, (count, count), 0) == lax.broadcasted_iota(jnp.int32, (count, count), 1)
        return jnp.sum(jnp.where(at, spread, 0), axis=1, keepdims=True)

    oi_ref[...] = upright(occ_lanes[...], OT)
    vb_ref[...] = upright(virt_lanes[...], VT)
    for a in range(VL):
        ml_ref[:, a * OT : (a + 1) * OT] = occ_lanes[...] ^ virt_ref[row * VL + a]
    for a in range(VC):
        vl_ref[:, a * VT : (a + 1) * VT] = virt_lanes[...] ^ virt_ref[col * VC + a]

    def l_step(a, carry):
        rows = pl.ds(pl.multiple_of(a * VT, VT), VT)
        labels = vb_ref[...] ^ virt_ref[row * VL + a]
        lmask[rows, :] = jnp.where(labels == vl_ref[...], l_ref[rows, :], 0.0)
        return carry

    lax.fori_loop(0, VL, l_step, 0)
    lx[core, z, yme] = lmask[...].T

    for a in range(VL):
        row_e[:, a * VT : (a + 1) * VT] = ve_lanes[...] + ve_ref[row * VL + a]
    for i in range(OL):
        col_e[:, i * OT : (i + 1) * OT] = oe_lanes[...] + oe_ref[col * OL + i]
    load_t.wait()
    for h in range(2):
        high, low = split2(tt[h])
        part_s = dot_nt(p_ref[...], high) + dot_nt(p_ref[...], low)
        for i in range(OL // 2):
            to = (h * 3 + i) * OT
            s_ref[:, to : to + OT] = part_s[:, i * OT : (i + 1) * OT]
    pl.semaphore_wait(bar, 21)

    def peer(ref, index):
        return ref.at[pl.ds(pl.multiple_of(index * 32, 32), 32), :]

    def a2a_copy(d):
        return rc(peer(s_ref, col ^ d), peer(raw, col), A2A + d, (row, col ^ d))

    yt = rc(tt_ref.at[1 - yh], tx.at[x, yh], YT, opp)
    yt.start()
    x1 = [rc(tt_ref.at[yh], tx.at[x, yh], X1 + n, dev) for n, dev in enumerate((right, left))]
    for copy in x1:
        copy.start()
    lax.fori_loop(1, 16, lambda d, n: (a2a_copy(d).start(), n)[1], 0)
    own_t = pltpu.make_async_copy(tt_ref.at[yh], tx.at[x, yh], lsem.at[0])
    own_t.start()
    own_s = pltpu.make_async_copy(peer(s_ref, col), peer(raw, col), lsem.at[1])
    own_s.start()
    own_l = lx.at[core, z, yme]
    ydevs = [(row, ycol), (yrow, ycol), opp]
    yidx = [yh * 2 + 1 - yl, (1 - yh) * 2 + 1 - yl, (1 - yh) * 2 + yl]
    ly = [rc(own_l, own_l, LY + n, dev) for n, dev in enumerate(ydevs)]
    for copy in ly:
        copy.start()
    lz = [rc(own_l, own_l, LZ + n, dev) for n, dev in enumerate((up, down))]
    for copy in lz:
        copy.start()

    order = [(xo, 1 - yh), (xo, yh), (xm, 1 - yh), (xp, 1 - yh), (xp, yh), (xm, yh), (x, 1 - yh), (x, yh)]

    def w_copy(t):
        dx, dy = order[t]
        return pltpu.make_async_copy(w_ref.at[dy * 4 + dx], wbuf.at[t % 2], wsem.at[t % 2])

    w_copy(0).start()
    w_copy(1).start()

    def w_split(t):
        dx, dy = order[t]
        own = ml_ref[...]

        def step(a, carry):
            rows = pl.ds(pl.multiple_of(a * OT, OT), OT)
            labels = oi_ref[...] ^ virt_ref[(dy * 4 + dx) * VL + a]
            kept = jnp.where(labels == own, wbuf[t % 2, rows, :], 0.0)
            high, low = split2(kept)
            w_hi[rows, :] = high
            w_lo[rows, :] = low
            return carry

        lax.fori_loop(0, VL, step, 0)

    def w_mm(t):
        def step(n, carry):
            rows = pl.ds(pl.multiple_of(n * 256, 256), 256)
            high, low = w_hi[rows, :], w_lo[rows, :]
            part[t, rows, :] = dot(high, ca_hi[...]) + dot(high, ca_lo[...]) + dot(low, ca_hi[...])
            return carry

        lax.fori_loop(0, CK // 256, step, 0)

    def cyc(t):
        if t > 0:
            w_copy(t).wait()
            w_split(t)
            if t + 2 < 8:
                w_copy(t + 2).start()
        w_mm(t)

    def add_into(dst, src):
        def step(n, carry):
            rows = pl.ds(pl.multiple_of(n * 96, 96), 96)
            dst[rows, :] = dst[rows, :] + src[rows, :]
            return carry

        lax.fori_loop(0, CK // 96, step, 0)

    w_copy(0).wait()
    w_split(0)
    w_copy(2).start()

    own_t.wait()
    yt.wait_send()
    pltpu.make_async_remote_copy(
        src_ref=tt_ref.at[1 - yh], dst_ref=tx.at[x, 1 - yh], send_sem=ssem.at[YT], recv_sem=rsem.at[YT],
        device_id=opp, device_id_type=MESH,
    ).wait_recv()
    x1b = [rc(tx.at[x, 1 - yh], tx.at[x, 1 - yh], X1 + 2 + n, dev) for n, dev in enumerate((right, left))]
    for copy in x1b:
        copy.start()

    x2 = []

    def pass_on(h, late):
        base = X1 + 2 * late
        rc(tx.at[xm, h], tx.at[xm, h], base, left).wait_recv()
        rc(tx.at[xp, h], tx.at[xp, h], base + 1, right).wait_recv()
        for n, (sx, rows, dev) in enumerate(((xm, upper, right), (xp, lower, left))):
            copy = rc(tx.at[sx, h, rows], tx.at[sx, h, rows], X2 + 2 * late + n, dev)
            copy.start()
            x2.append(copy)

    upper, lower = pl.ds(0, HIJ // 2), pl.ds(HIJ // 2, HIJ // 2)
    pass_on(yh, 0)

    own_s.wait()

    def a2a_wait(d, carry):
        a2a_copy(d).wait_send()
        rc(peer(s_ref, col), peer(raw, col ^ d), A2A + d, (row, col ^ d)).wait_recv()
        return carry

    lax.fori_loop(1, 16, a2a_wait, 0)

    def ca_step(c, carry):
        for i in range(OL):
            parts = [
                raw[pl.ds(pl.multiple_of(c * 32 + b * VL, VL), VL), i * OT : (i + 1) * OT] for b in range(VC)
            ]
            wide = jnp.concatenate(parts, axis=1)
            for n in range(3):
                ca[n, pl.ds(c * OL + i, VL, stride=OT), :] = wide[:, n * THIRD : (n + 1) * THIRD]
        return carry

    lax.fori_loop(0, 16, ca_step, 0)
    for n in range(3):
        high, low = split2(ca[n])
        ca_hi[:, n * THIRD : (n + 1) * THIRD] = high
        ca_lo[:, n * THIRD : (n + 1) * THIRD] = low

    rs = [
        rc(part.at[0], recv.at[0], RS + 0, right),
        rc(part.at[1], recv.at[1], RS + 1, left),
    ]
    lanes3 = [pl.ds(n * THIRD, THIRD) for n in range(3)]
    slot_dev = {2: left, 3: right, 4: right, 5: left}
    rs3 = {
        t: [
            rc(part.at[t, :, lanes], recv.at[t, :, lanes], RS + 2 + (t - 2) * 3 + n, slot_dev[t])
            for n, lanes in enumerate(lanes3)
        ]
        for t in slot_dev
    }

    def send3(t):
        for copy in rs3[t]:
            copy.start()

    cyc(0)
    rs[0].start()
    cyc(1)
    rs[1].start()

    for n, dst_y in enumerate(yidx):
        ly[n].wait_send()
        block = lx.at[core, z, dst_y]
        rc(own_l, block, LY + n, ydevs[n]).wait_recv()
        for m, dev in enumerate((up, down)):
            copy = rc(block, block, LZ + 2 + 2 * n + m, dev)
            copy.start()
            lz.append(copy)
    lc = [rc(lx.at[core, zz], lx.at[core, zz], LC + n, mate) for n, zz in enumerate((z, zm, zp, zo))]
    lc[0].start()

    cyc(2)
    send3(2)
    cyc(3)
    rs[0].wait_recv()
    add_into(part.at[3], recv.at[0])
    send3(3)
    pass_on(1 - yh, 1)
    cyc(4)
    send3(4)
    cyc(5)
    rs[1].wait_recv()
    add_into(part.at[5], recv.at[1])
    send3(5)

    for n, src_y in enumerate([yme] + yidx):
        rc(lx.at[core, zm, src_y], lx.at[core, zm, src_y], LZ + 2 * n, down).wait_recv()
        rc(lx.at[core, zp, src_y], lx.at[core, zp, src_y], LZ + 2 * n + 1, up).wait_recv()
    lz2 = [
        rc(lx.at[core, zm, pl.ds(0, 2)], lx.at[core, zm, pl.ds(0, 2)], LZ2 + 0, up),
        rc(lx.at[core, zp, pl.ds(2, 2)], lx.at[core, zp, pl.ds(2, 2)], LZ2 + 1, down),
    ]
    for copy in lz2:
        copy.start()
    lc[1].start()
    lc[2].start()

    cyc(6)
    cyc(7)

    yr = []
    for n, lanes in enumerate(lanes3):
        rs3[3][n].wait_recv()
        rs3[2][n].wait_recv()
        part[6, :, lanes] = part[6, :, lanes] + (recv[3, :, lanes] + recv[2, :, lanes])
        copy = rc(part.at[6, :, lanes], yrecv.at[:, lanes], YR + n, opp)
        copy.start()
        yr.append(copy)

    rc(lx.at[core, zo, pl.ds(0, 2)], lx.at[core, zo, pl.ds(0, 2)], LZ2 + 0, down).wait_recv()
    rc(lx.at[core, zo, pl.ds(2, 2)], lx.at[core, zo, pl.ds(2, 2)], LZ2 + 1, up).wait_recv()
    lc[3].start()
    for n, zz in enumerate((z, zm, zp, zo)):
        rc(lx.at[1 - core, zz], lx.at[1 - core, zz], LC + n, mate).wait_recv()

    for h in range(2):
        oacc[h] = jnp.zeros((HIJ, AB), F32)

    def ladder(sx, n):
        kc, sy = n // 2, n % 2
        source = sy * 4 + sx
        zz, ylo = source // 2, source % 2
        lanes = pl.ds(pl.multiple_of(kc * CD, CD), CD)
        t_hi, t_lo = split2(tx[sx, sy, :, lanes])
        both = jnp.concatenate([t_hi, t_lo], axis=0)
        for h in range(2):
            high, low = split2(lx[kc, zz, h * 2 + ylo])
            wide = dot(both, high)
            oacc[h] = oacc[h] + (wide[:HIJ] + wide[HIJ:] + dot(t_hi, low))

    def ladder_run(sx):
        lax.fori_loop(0, 4, lambda n, carry: (ladder(sx, n), carry)[1], 0)

    def back_copy(n, d):
        return rc(
            cp.at[col ^ d, :, lanes3[n]], d_ref.at[col, :, lanes3[n]], BACK + 16 * n + d, (row, col ^ d)
        )

    own_d = [
        pltpu.make_async_copy(cp.at[col, :, lanes], d_ref.at[col, :, lanes], lsem.at[1 + n])
        for n, lanes in enumerate(lanes3)
    ]

    def finish(n):
        lanes = lanes3[n]
        rs3[4][n].wait_recv()
        rs3[5][n].wait_recv()
        yr[n].wait_recv()
        value = (part[7, :, lanes] + recv[4, :, lanes]) + (recv[5, :, lanes] + yrecv[:, lanes])
        high, low = split2(value)
        rest = (value - high.astype(F32) - low.astype(F32)).astype(BF16)
        sel = q_ref[...]
        cp[:, :, lanes] = (dot(sel, high) + dot(sel, low) + dot(sel, rest)).reshape(16, BLK, THIRD)
        lax.fori_loop(1, 16, lambda d, carry: (back_copy(n, d).start(), carry)[1], 0)
        own_d[n].start()

    ladder_run(x)
    ladder_run(xm)
    ladder_run(xp)
    finish(0)
    for base, sx, rows, dev in ((0, xo, upper, left), (1, xo, lower, right)):
        for h, late in ((yh, 0), (1 - yh, 1)):
            rc(tx.at[sx, h, rows], tx.at[sx, h, rows], X2 + 2 * late + base, dev).wait_recv()
    ladder_run(xo)
    out_own = pltpu.make_async_copy(oacc.at[yh], lo_ref.at[yh], lsem.at[0])
    out_own.start()
    ob = rc(oacc.at[1 - yh], lo_ref.at[yh], OB, opp)
    ob.start()
    finish(1)
    finish(2)

    for copy in x1 + x1b + x2 + lz + lz2 + lc + rs + sum(rs3.values(), []) + yr + [ob]:
        copy.wait_send()
    rc(oacc.at[yh], lo_ref.at[1 - yh], OB, opp).wait_recv()
    out_own.wait()
    for n, lanes in enumerate(lanes3):
        own_d[n].wait()

        def back_wait(d, carry):
            back_copy(n, d).wait_send()
            rc(
                cp.at[col, :, lanes], d_ref.at[col ^ d, :, lanes], BACK + 16 * n + d, (row, col ^ d)
            ).wait_recv()
            return carry

        lax.fori_loop(1, 16, back_wait, 0)


def to_peers():
    c, b, a = np.meshgrid(np.arange(16), np.arange(VC), np.arange(VL), indexing="ij")
    table = np.zeros((AB, AB), np.float32)
    table[(c * 32 + b * VL + a).reshape(-1), (a * VT + c * VC + b).reshape(-1)] = 1.0
    return table


def from_cycle():
    a, c, i = np.meshgrid(np.arange(VL), np.arange(16), np.arange(OL), indexing="ij")
    table = np.zeros((CK, CK), np.float32)
    table[(c * BLK + a * OL + i).reshape(-1), (a * OT + c * OL + i).reshape(-1)] = 1.0
    return table


def body(amps, ladder_ints, cycle_ints, virt_irrep, occ_irrep, virt_energy, occ_energy):
    turned = amps.T.reshape(2, HIJ, AB)
    anywhere = pl.BlockSpec(memory_space=pl.ANY)
    vmem = pl.BlockSpec(memory_space=pltpu.VMEM)
    smem = pl.BlockSpec(memory_space=pltpu.SMEM)
    ladder, cycle, row_energy, col_energy = pl.pallas_call(
        kernel,
        out_shape=(
            jax.ShapeDtypeStruct((2, HIJ, AB), F32),
            jax.ShapeDtypeStruct((16, BLK, BJ), F32),
            jax.ShapeDtypeStruct((1, AB), F32),
            jax.ShapeDtypeStruct((1, OL * OT), F32),
        ),
        in_specs=[smem] * 3 + [anywhere, vmem, anywhere] + [vmem] * 6,
        out_specs=(anywhere, anywhere, vmem, vmem),
        scratch_shapes=[
            pltpu.VMEM((2, HIJ, AB), F32),
            pltpu.VMEM((AB, OL * OT), F32),
            pltpu.VMEM((4, 2, HIJ, AB), F32),
            pltpu.VMEM((2, 4, 4, CD, AB), F32),
            pltpu.VMEM((AB, OL * OT), F32),
            pltpu.VMEM((3, CK, THIRD), F32),
            pltpu.VMEM((CK, BJ), BF16),
            pltpu.VMEM((CK, BJ), BF16),
            pltpu.VMEM((2, CK, CK), F32),
            pltpu.VMEM((CK, CK), BF16),
            pltpu.VMEM((CK, CK), BF16),
            pltpu.VMEM((8, CK, BJ), F32),
            pltpu.VMEM((6, CK, BJ), F32),
            pltpu.VMEM((CK, BJ), F32),
            pltpu.VMEM((2, HIJ, AB), F32),
            pltpu.VMEM((AB, CD), F32),
            pltpu.VMEM((16, BLK, BJ), F32),
            pltpu.VMEM((1, CK), jnp.int32),
            pltpu.VMEM((1, CD), jnp.int32),
            pltpu.VMEM((OT, 1), jnp.int32),
            pltpu.VMEM((VT, 1), jnp.int32),
            pltpu.SemaphoreType.DMA((NSEM,)),
            pltpu.SemaphoreType.DMA((NSEM,)),
            pltpu.SemaphoreType.DMA((2,)),
            pltpu.SemaphoreType.DMA((4,)),
        ],
        compiler_params=pltpu.CompilerParams(
            collective_id=0, has_side_effects=True, vmem_limit_bytes=67043328
        ),
    )(
        virt_irrep, virt_energy, occ_energy, turned, ladder_ints, cycle_ints.reshape(8, CK, CK),
        virt_irrep.reshape(1, VT), occ_irrep.reshape(1, OT), virt_energy.reshape(1, VT), occ_energy.reshape(1, OT),
        jnp.asarray(to_peers(), BF16), jnp.asarray(from_cycle(), BF16),
    )
    back = cycle.reshape(16, VL, OL, VC, OT).transpose(2, 4, 1, 0, 3).reshape(OL * OT, AB)
    return ((ladder.reshape(OL * OT, AB) + back) / (row_energy - col_energy.reshape(OL * OT, 1))).T


def solution(mesh):
    placed = (P("row", "col"), P("row", "col"), P(None, "row"), P(), P(), P(), P())
    return jax.shard_map(
        body, mesh=mesh, in_specs=placed, out_specs=P("row", "col"), check_vma=False
    )
```

```python
import functools

import jax
import jax.numpy as jnp
import numpy as np
from jax import lax
from jax.experimental import pallas as pl
from jax.experimental.pallas import tpu as pltpu
from jax.sharding import PartitionSpec as P

MESH = pl.DeviceIdType.MESH
F32, BF16 = jnp.float32, jnp.bfloat16

VT, OT = 64, 96
VL, OL, VC = 8, 6, 4
CK = VL * OT
BJ = VC * OT
BLK = VL * OL
THIRD = BJ // 3
AB = VL * VT
CD = 256
HIJ = OL * OT // 2

A2A, BACK, YT, X1, X2, LY = 0, 16, 64, 65, 69, 73
LZ, LZ2, LC, OB, RS, YR, LY2 = 76, 84, 92, 96, 97, 114, 117
NSEM = 119


def split2(value):
    high = value.astype(BF16)
    low = (value - high.astype(F32)).astype(BF16)
    return high, low


def dot_nt(a, b):
    return lax.dot_general(a, b, (((1,), (1,)), ((), ())), preferred_element_type=F32)


def dot(a, b):
    return jnp.dot(a, b, preferred_element_type=F32)


def kernel(
    virt_ref, ve_ref, oe_ref, tt_ref, l_ref, w_ref, virt_lanes, occ_lanes, ve_lanes, oe_lanes, p_ref, q_ref,
    out_ref,
    row_s, oe_up, lad, tt, s_ref, tx, lx, raw, ca, ca_hi, ca_lo, wbuf, w_hi, w_lo, part, recv, yrecv, oacc, lmask, cp, d3, ml_ref, vl_ref, oi_ref, vb_ref,
    ssem, rsem, wsem, lsem,
):
    row, col = lax.axis_index("row"), lax.axis_index("col")
    yh, x = row // 4, row % 4
    z, yl, core = col // 4, (col // 2) % 2, col % 2
    yme = yh * 2 + yl
    xp, xm, xo = (x + 1) % 4, (x + 3) % 4, (x + 2) % 4
    zp, zm, zo = (z + 1) % 4, (z + 3) % 4, (z + 2) % 4
    right, left = (yh * 4 + xp, col), (yh * 4 + xm, col)
    up, down = (row, zp * 4 + col % 4), (row, zm * 4 + col % 4)
    yrow = (1 - yh) * 4 + x
    ycol = z * 4 + (1 - yl) * 2 + core
    opp = (yrow, col)
    mate = (row, z * 4 + yl * 2 + (1 - core))

    def rc(src, dst, k, dev):
        return pltpu.make_async_remote_copy(
            src_ref=src, dst_ref=dst, send_sem=ssem.at[k], recv_sem=rsem.at[k],
            device_id=dev, device_id_type=MESH,
        )

    bar = pltpu.get_barrier_semaphore()

    def greet(d, carry):
        pl.semaphore_signal(bar, inc=1, device_id=(row, col ^ d), device_id_type=MESH)
        return carry

    lax.fori_loop(1, 16, greet, 0)
    for dev in (right, left, up, down, opp, (yrow, ycol)):
        pl.semaphore_signal(bar, inc=1, device_id=dev, device_id_type=MESH)

    load_t = pltpu.make_async_copy(tt_ref, tt, lsem.at[0])
    load_t.start()

    def upright(lanes, count):
        spread = jnp.broadcast_to(lanes, (count, count))
        at = lax.broadcasted_iota(jnp.int32, (count, count), 0) == lax.broadcasted_iota(jnp.int32, (count, count), 1)
        return jnp.sum(jnp.where(at, spread, jnp.zeros_like(spread)), axis=1, keepdims=True)

    oi_ref[...] = upright(occ_lanes[...], OT)
    vb_ref[...] = upright(virt_lanes[...], VT)
    for a in range(VL):
        ml_ref[:, a * OT : (a + 1) * OT] = occ_lanes[...] ^ virt_ref[row * VL + a]
    for a in range(VC):
        vl_ref[:, a * VT : (a + 1) * VT] = virt_lanes[...] ^ virt_ref[col * VC + a]

    def l_step(a, carry):
        rows = pl.ds(pl.multiple_of(a * VT, VT), VT)
        labels = vb_ref[...] ^ virt_ref[row * VL + a]
        lmask[rows, :] = jnp.where(labels == vl_ref[...], l_ref[rows, :], 0.0)
        return carry

    lax.fori_loop(0, VL, l_step, 0)
    lx[core, z, yme] = lmask[...].T

    for a in range(VL):
        row_s[:, a * VT : (a + 1) * VT] = ve_lanes[...] + ve_ref[row * VL + a]
    oe_up[...] = upright(oe_lanes[...], OT)
    load_t.wait()
    for h in range(2):
        high, low = split2(tt[h])
        part_s = dot_nt(p_ref[...], high) + dot_nt(p_ref[...], low)
        for i in range(OL // 2):
            to = (h * 3 + i) * OT
            s_ref[:, to : to + OT] = part_s[:, i * OT : (i + 1) * OT]
    pl.semaphore_wait(bar, 21)

    def peer(ref, index):
        return ref.at[pl.ds(pl.multiple_of(index * 32, 32), 32), :]

    def a2a_copy(d):
        return rc(peer(s_ref, col ^ d), peer(raw, col), A2A + d, (row, col ^ d))

    yt = rc(tt_ref.at[1 - yh], tx.at[x, yh], YT, opp)
    yt.start()
    x1 = [rc(tt_ref.at[yh], tx.at[x, yh], X1 + n, dev) for n, dev in enumerate((right, left))]
    for copy in x1:
        copy.start()
    lax.fori_loop(1, 16, lambda d, n: (a2a_copy(d).start(), n)[1], 0)
    own_t = pltpu.make_async_copy(tt_ref.at[yh], tx.at[x, yh], lsem.at[0])
    own_t.start()
    own_s = pltpu.make_async_copy(peer(s_ref, col), peer(raw, col), lsem.at[1])
    own_s.start()
    own_l = lx.at[core, z, yme]
    ydevs = [(row, ycol), (yrow, ycol), opp]
    yidx = [yh * 2 + 1 - yl, (1 - yh) * 2 + 1 - yl, (1 - yh) * 2 + yl]
    ly = [rc(own_l, own_l, LY + n, dev) for n, dev in enumerate(ydevs[:2])]
    ly[0].start()
    ly[1].start()
    lz = [rc(own_l, own_l, LZ + n, dev) for n, dev in enumerate((up, down))]
    for copy in lz:
        copy.start()

    order = [(xp, 1 - yh), (xm, 1 - yh), (xo, 1 - yh), (xo, yh), (xp, yh), (xm, yh), (x, 1 - yh), (x, yh)]

    def w_copy(t):
        dx, dy = order[t]
        return pltpu.make_async_copy(w_ref.at[dy * 4 + dx], wbuf.at[t % 2], wsem.at[t % 2])

    w_copy(0).start()
    w_copy(1).start()

    def w_split(t):
        dx, dy = order[t]
        own = ml_ref[...]

        def step(a, carry):
            rows = pl.ds(pl.multiple_of(a * OT, OT), OT)
            labels = oi_ref[...] ^ virt_ref[(dy * 4 + dx) * VL + a]
            kept = jnp.where(labels == own, wbuf[t % 2, rows, :], 0.0)
            high, low = split2(kept)
            w_hi[rows, :] = high
            w_lo[rows, :] = low
            return carry

        lax.fori_loop(0, VL, step, 0)

    def w_mm(t):
        def step(n, carry):
            rows = pl.ds(pl.multiple_of(n * 256, 256), 256)
            high, low = w_hi[rows, :], w_lo[rows, :]
            part[t, rows, :] = dot(high, ca_hi[...]) + dot(high, ca_lo[...]) + dot(low, ca_hi[...])
            return carry

        lax.fori_loop(0, CK // 256, step, 0)

    def cyc(t):
        if t > 0:
            w_copy(t).wait()
            w_split(t)
            if t + 2 < 8:
                w_copy(t + 2).start()
        w_mm(t)

    def add_into(dst, src):
        def step(n, carry):
            rows = pl.ds(pl.multiple_of(n * 96, 96), 96)
            dst[rows, :] = dst[rows, :] + src[rows, :]
            return carry

        lax.fori_loop(0, CK // 96, step, 0)

    w_copy(0).wait()
    w_split(0)
    w_copy(2).start()

    own_t.wait()
    yt.wait_send()
    pltpu.make_async_remote_copy(
        src_ref=tt_ref.at[1 - yh], dst_ref=tx.at[x, 1 - yh], send_sem=ssem.at[YT], recv_sem=rsem.at[YT],
        device_id=opp, device_id_type=MESH,
    ).wait_recv()
    x1b = [rc(tx.at[x, 1 - yh], tx.at[x, 1 - yh], X1 + 2 + n, dev) for n, dev in enumerate((right, left))]
    for copy in x1b:
        copy.start()

    x2 = []

    def pass_on(h, late):
        base = X1 + 2 * late
        rc(tx.at[xm, h], tx.at[xm, h], base, left).wait_recv()
        rc(tx.at[xp, h], tx.at[xp, h], base + 1, right).wait_recv()
        for n, (sx, rows, dev) in enumerate(((xm, upper, right), (xp, lower, left))):
            copy = rc(tx.at[sx, h, rows], tx.at[sx, h, rows], X2 + 2 * late + n, dev)
            copy.start()
            x2.append(copy)

    upper, lower = pl.ds(0, HIJ // 2), pl.ds(HIJ // 2, HIJ // 2)
    pass_on(yh, 0)

    lz2 = []

    def pass_block(n, src_y):
        rc(lx.at[core, zm, src_y], lx.at[core, zm, src_y], LZ + 2 * n, down).wait_recv()
        rc(lx.at[core, zp, src_y], lx.at[core, zp, src_y], LZ + 2 * n + 1, up).wait_recv()
        for m, (sz, first, dev) in enumerate(((zm, 0, up), (zp, CD // 2, down))):
            piece = lx.at[core, sz, src_y, pl.ds(first, CD // 2)]
            copy = rc(piece, piece, LZ2 + 2 * n + m, dev)
            copy.start()
            lz2.append(copy)

    pass_block(0, yme)

    own_s.wait()

    def a2a_wait(d, carry):
        a2a_copy(d).wait_send()
        rc(peer(s_ref, col), peer(raw, col ^ d), A2A + d, (row, col ^ d)).wait_recv()
        return carry

    lax.fori_loop(1, 16, a2a_wait, 0)

    def ca_step(c, carry):
        for i in range(OL):
            parts = [
                raw[pl.ds(pl.multiple_of(c * 32 + b * VL, VL), VL), i * OT : (i + 1) * OT] for b in range(VC)
            ]
            wide = jnp.concatenate(parts, axis=1)
            for n in range(3):
                ca[n, pl.ds(c * OL + i, VL, stride=OT), :] = wide[:, n * THIRD : (n + 1) * THIRD]
        return carry

    lax.fori_loop(0, 16, ca_step, 0)
    for n in range(3):
        high, low = split2(ca[n])
        ca_hi[:, n * THIRD : (n + 1) * THIRD] = high
        ca_lo[:, n * THIRD : (n + 1) * THIRD] = low

    lanes3 = [pl.ds(n * THIRD, THIRD) for n in range(3)]
    top, bottom = pl.ds(0, CK // 2), pl.ds(CK // 2, CK // 2)
    direct = [
        rc(part.at[0], recv.at[0], RS + 0, right),
        rc(part.at[1], recv.at[1], RS + 1, left),
        rc(part.at[2], recv.at[2], RS + 2, opp),
        rc(part.at[4, bottom], recv.at[4, bottom], RS + 3, right),
        rc(part.at[5, top], recv.at[5, top], RS + 4, left),
    ]
    first_hop = [
        [
            rc(part.at[3, rows, lanes], recv.at[3, rows, lanes], RS + 5 + 3 * m + n, dev)
            for m, (rows, dev) in enumerate(((top, right), (bottom, left)))
        ]
        for n, lanes in enumerate(lanes3)
    ]
    second_hop = [
        [
            rc(part.at[t, rows, lanes], recv.at[t, rows, lanes], RS + 11 + 3 * m + n, dev)
            for m, (t, rows, dev) in enumerate(((4, top, right), (5, bottom, left)))
        ]
        for n, lanes in enumerate(lanes3)
    ]
    mine, other = [pl.ds(pl.multiple_of(h * (CD // 2), CD // 2), CD // 2) for h in (yh, 1 - yh)]

    def over_z(n):
        block = lx.at[core, z, yidx[n]]
        if n < 2:
            rc(own_l, block, LY + n, ydevs[n]).wait_recv()
            piece = lx.at[core, z, yidx[n], mine]
            copy = rc(piece, piece, LY2 + n, ydevs[1 - n])
            copy.start()
            ly.append(copy)
        else:
            for m, rows in ((0, other), (1, mine)):
                piece = lx.at[core, z, yidx[n], rows]
                rc(piece, piece, LY2 + m, ydevs[1 - m]).wait_recv()
        for m, dev in enumerate((up, down)):
            copy = rc(block, block, LZ + 2 + 2 * n + m, dev)
            copy.start()
            lz.append(copy)

    cyc(0)
    direct[0].start()
    pass_on(1 - yh, 1)
    over_z(0)
    over_z(1)
    cyc(1)
    direct[1].start()
    cyc(2)
    direct[2].start()

    over_z(2)
    lc = [rc(lx.at[core, zz], lx.at[core, zz], LC + n, mate) for n, zz in enumerate((z, zm, zp, zo))]
    lc[0].start()

    cyc(3)
    cyc(4)
    direct[3].start()
    cyc(5)
    direct[4].start()
    pass_block(1, yidx[0])
    pass_block(2, yidx[1])
    cyc(6)
    cyc(7)

    direct[0].wait_recv()
    direct[1].wait_recv()
    yr = []
    for n, lanes in enumerate(lanes3):
        part[6, :, lanes] = part[6, :, lanes] + (recv[0, :, lanes] + recv[1, :, lanes])
        copy = rc(part.at[6, :, lanes], yrecv.at[:, lanes], YR + n, opp)
        copy.start()
        yr.append(copy)

    pass_block(3, yidx[2])
    lc[1].start()
    lc[2].start()

    direct[2].wait_recv()
    for n, lanes in enumerate(lanes3):
        part[3, :, lanes] = part[3, :, lanes] + recv[2, :, lanes]
        for copy in first_hop[n]:
            copy.start()

    def relay(n):
        lanes = lanes3[n]
        for m, (t, rows) in enumerate(((4, top), (5, bottom))):
            first_hop[n][m].wait_recv()
            part[t, rows, lanes] = part[t, rows, lanes] + recv[3, rows, lanes]
            second_hop[n][m].start()

    relay(0)
    relay(1)

    for n, src_y in enumerate([yme] + yidx):
        for m, (first, dev) in enumerate(((0, down), (CD // 2, up))):
            piece = lx.at[core, zo, src_y, pl.ds(first, CD // 2)]
            rc(piece, piece, LZ2 + 2 * n + m, dev).wait_recv()
    lc[3].start()

    for h in range(2):
        oacc[h] = jnp.zeros((HIJ, AB), F32)

    def ladder(sx, kc, sy):
        source = sy * 4 + sx
        zz, ylo = source // 2, source % 2
        lanes = pl.ds(pl.multiple_of(kc * CD, CD), CD)
        t_hi, t_lo = split2(tx[sx, sy, :, lanes])
        both = jnp.concatenate([t_hi, t_lo], axis=0)
        for h in range(2):
            high, low = split2(lx[kc, zz, h * 2 + ylo])
            wide = dot(both, high)
            oacc[h] = oacc[h] + (wide[:HIJ] + wide[HIJ:] + dot(t_hi, low))

    def ladder_run(kc):
        lax.fori_loop(0, 8, lambda n, carry: (ladder(n % 4, kc, n // 4), carry)[1], 0)

    def back_copy(n, d):
        return rc(
            cp.at[n, col ^ d], d3.at[n, col], BACK + 16 * n + d, (row, col ^ d)
        )

    own_d = [
        pltpu.make_async_copy(cp.at[n, col], d3.at[n, col], lsem.at[1 + n])
        for n, lanes in enumerate(lanes3)
    ]

    def finish(n):
        lanes = lanes3[n]
        for copy in second_hop[n] + [yr[n]]:
            copy.wait_recv()
        if n == 0:
            direct[3].wait_recv()
            direct[4].wait_recv()
        value = (part[7, :, lanes] + recv[4, :, lanes]) + (recv[5, :, lanes] + yrecv[:, lanes])
        high, low = split2(value)
        rest = (value - high.astype(F32) - low.astype(F32)).astype(BF16)
        sel = q_ref[...]
        cp[n] = (dot(sel, high) + dot(sel, low) + dot(sel, rest)).reshape(16, BLK, THIRD)
        lax.fori_loop(1, 16, lambda d, carry: (back_copy(n, d).start(), carry)[1], 0)
        own_d[n].start()

    for base, rows, dev in ((0, upper, left), (1, lower, right)):
        for h, late in ((yh, 0), (1 - yh, 1)):
            rc(tx.at[xo, h, rows], tx.at[xo, h, rows], X2 + 2 * late + base, dev).wait_recv()
    ladder_run(core)
    relay(2)
    finish(0)
    for n, zz in enumerate((z, zm, zp, zo)):
        rc(lx.at[1 - core, zz], lx.at[1 - core, zz], LC + n, mate).wait_recv()
    ladder_run(1 - core)
    out_own = pltpu.make_async_copy(oacc.at[yh], lad.at[yh], lsem.at[0])
    out_own.start()
    ob = rc(oacc.at[1 - yh], lad.at[yh], OB, opp)
    ob.start()
    finish(1)
    finish(2)

    for copy in x1 + x1b + x2 + ly + lz + lz2 + lc + direct + sum(first_hop + second_hop, []) + yr + [ob]:
        copy.wait_send()
    rc(oacc.at[yh], lad.at[1 - yh], OB, opp).wait_recv()
    out_own.wait()
    def unpack(c):
        wide = [
            jnp.concatenate([d3[n, c, pl.ds(i, VL, stride=OL), :] for n in range(3)], axis=1) for i in range(OL)
        ]
        for b in range(VC):
            rows = pl.ds(pl.multiple_of(c * 32 + b * VL, VL), VL)
            raw[rows, :] = jnp.concatenate([value[:, b * OT : (b + 1) * OT] for value in wide], axis=1)

    for n in range(3):
        own_d[n].wait()

        def back_wait(d, carry):
            leaving = back_copy(n, d)
            leaving.wait_send()
            arriving = rc(cp.at[n, col], d3.at[n, col ^ d], BACK + 16 * n + d, (row, col ^ d))
            arriving.wait_recv()
            if n == 2:
                unpack(col ^ d)
            return carry

        if n == 2:
            unpack(col)
        lax.fori_loop(1, 16, back_wait, 0)

    turned = raw[...].T
    tt[0] = turned[:HIJ]
    tt[1] = turned[HIJ:]
    for i in range(OL):
        h, rows = i // 3, pl.ds((i % 3) * OT, OT)
        value = tt[h, rows, :]
        high, low = split2(value)
        rest = (value - high.astype(F32) - low.astype(F32)).astype(BF16)
        sel = p_ref[...]
        total = lad[h, rows, :] + (dot(high, sel) + dot(low, sel) + dot(rest, sel))
        out_ref[i * OT : (i + 1) * OT, :] = total / (row_s[...] - (oe_up[...] + oe_ref[col * OL + i]))


def to_peers():
    c, b, a = np.meshgrid(np.arange(16), np.arange(VC), np.arange(VL), indexing="ij")
    table = np.zeros((AB, AB), np.float32)
    table[(c * 32 + b * VL + a).reshape(-1), (a * VT + c * VC + b).reshape(-1)] = 1.0
    return table


def from_cycle():
    a, c, i = np.meshgrid(np.arange(VL), np.arange(16), np.arange(OL), indexing="ij")
    table = np.zeros((CK, CK), np.float32)
    table[(c * BLK + a * OL + i).reshape(-1), (a * OT + c * OL + i).reshape(-1)] = 1.0
    return table


def body(amps, ladder_ints, cycle_ints, virt_irrep, occ_irrep, virt_energy, occ_energy):
    turned = amps.T.reshape(2, HIJ, AB)
    anywhere = pl.BlockSpec(memory_space=pl.ANY)
    vmem = pl.BlockSpec(memory_space=pltpu.VMEM)
    smem = pl.BlockSpec(memory_space=pltpu.SMEM)
    update = pl.pallas_call(
        kernel,
        out_shape=jax.ShapeDtypeStruct((OL * OT, AB), F32),
        in_specs=[smem] * 3 + [anywhere, vmem, anywhere] + [vmem] * 6,
        out_specs=vmem,
        scratch_shapes=[
            pltpu.VMEM((1, AB), F32),
            pltpu.VMEM((OT, 1), F32),
            pltpu.VMEM((2, HIJ, AB), F32),
            pltpu.VMEM((2, HIJ, AB), F32),
            pltpu.VMEM((AB, OL * OT), F32),
            pltpu.VMEM((4, 2, HIJ, AB), F32),
            pltpu.VMEM((2, 4, 4, CD, AB), F32),
            pltpu.VMEM((AB, OL * OT), F32),
            pltpu.VMEM((3, CK, THIRD), F32),
            pltpu.VMEM((CK, BJ), BF16),
            pltpu.VMEM((CK, BJ), BF16),
            pltpu.VMEM((2, CK, CK), F32),
            pltpu.VMEM((CK, CK), BF16),
            pltpu.VMEM((CK, CK), BF16),
            pltpu.VMEM((8, CK, BJ), F32),
            pltpu.VMEM((6, CK, BJ), F32),
            pltpu.VMEM((CK, BJ), F32),
            pltpu.VMEM((2, HIJ, AB), F32),
            pltpu.VMEM((AB, CD), F32),
            pltpu.VMEM((3, 16, BLK, THIRD), F32),
            pltpu.VMEM((3, 16, BLK, THIRD), F32),
            pltpu.VMEM((1, CK), jnp.int32),
            pltpu.VMEM((1, CD), jnp.int32),
            pltpu.VMEM((OT, 1), jnp.int32),
            pltpu.VMEM((VT, 1), jnp.int32),
            pltpu.SemaphoreType.DMA((NSEM,)),
            pltpu.SemaphoreType.DMA((NSEM,)),
            pltpu.SemaphoreType.DMA((2,)),
            pltpu.SemaphoreType.DMA((6,)),
        ],
        compiler_params=pltpu.CompilerParams(
            collective_id=0, has_side_effects=True, vmem_limit_bytes=67043328
        ),
    )(
        virt_irrep, virt_energy, occ_energy, turned, ladder_ints, cycle_ints.reshape(8, CK, CK),
        virt_irrep.reshape(1, VT), occ_irrep.reshape(1, OT), virt_energy.reshape(1, VT), occ_energy.reshape(1, OT),
        jnp.asarray(to_peers(), BF16), jnp.asarray(from_cycle(), BF16),
    )
    return update.T


def solution(mesh):
    placed = (P("row", "col"), P("row", "col"), P(None, "row"), P(), P(), P(), P())
    return jax.shard_map(
        body, mesh=mesh, in_specs=placed, out_specs=P("row", "col"), check_vma=False
    )
```

```python
import functools

import jax
import jax.numpy as jnp
import numpy as np
from jax import lax
from jax.experimental import pallas as pl
from jax.experimental.pallas import tpu as pltpu
from jax.sharding import PartitionSpec as P

MESH = pl.DeviceIdType.MESH
F32, BF16 = jnp.float32, jnp.bfloat16

VT, OT = 64, 96
VL, OL, VC = 8, 6, 4
CK = VL * OT
BJ = VC * OT
BLK = VL * OL
THIRD = BJ // 3
AB = VL * VT
CD = 256
HIJ = OL * OT // 2

A2A, BACK, YT, X1, X2, LY = 0, 16, 64, 65, 69, 73
LZ, LZ2, LC, OB, RS, YR, LY2 = 76, 84, 92, 96, 97, 114, 117
NSEM = 119


def split2(value):
    high = value.astype(BF16)
    low = (value - high.astype(F32)).astype(BF16)
    return high, low


def dot_nt(a, b):
    return lax.dot_general(a, b, (((1,), (1,)), ((), ())), preferred_element_type=F32)


def dot(a, b):
    return jnp.dot(a, b, preferred_element_type=F32)


def kernel(
    virt_ref, ve_ref, oe_ref, tt_ref, l_ref, w_ref, virt_lanes, occ_lanes, ve_lanes, oe_lanes, p_ref, q_ref,
    out_ref,
    row_s, oe_up, lad, turned, tt, s_ref, tx, lx, raw, ca, ca_hi, ca_lo, wbuf, w_hi, w_lo, part, recv, yrecv, oacc, lmask, cp, d3, ml_ref, vl_ref, oi_ref, vb_ref,
    ssem, rsem, wsem, lsem, osem,
):
    row, col = lax.axis_index("row"), lax.axis_index("col")
    yh, x = row // 4, row % 4
    z, yl, core = col // 4, (col // 2) % 2, col % 2
    yme = yh * 2 + yl
    xp, xm, xo = (x + 1) % 4, (x + 3) % 4, (x + 2) % 4
    zp, zm, zo = (z + 1) % 4, (z + 3) % 4, (z + 2) % 4
    right, left = (yh * 4 + xp, col), (yh * 4 + xm, col)
    up, down = (row, zp * 4 + col % 4), (row, zm * 4 + col % 4)
    yrow = (1 - yh) * 4 + x
    ycol = z * 4 + (1 - yl) * 2 + core
    opp = (yrow, col)
    mate = (row, z * 4 + yl * 2 + (1 - core))

    def rc(src, dst, k, dev):
        return pltpu.make_async_remote_copy(
            src_ref=src, dst_ref=dst, send_sem=ssem.at[k], recv_sem=rsem.at[k],
            device_id=dev, device_id_type=MESH,
        )

    bar = pltpu.get_barrier_semaphore()

    def greet(d, carry):
        pl.semaphore_signal(bar, inc=1, device_id=(row, col ^ d), device_id_type=MESH)
        return carry

    lax.fori_loop(1, 16, greet, 0)
    for dev in (right, left, up, down, opp, (yrow, ycol)):
        pl.semaphore_signal(bar, inc=1, device_id=dev, device_id_type=MESH)

    load_t = pltpu.make_async_copy(tt_ref, tt, lsem.at[0])
    load_t.start()

    def upright(lanes, count):
        spread = jnp.broadcast_to(lanes, (count, count))
        at = lax.broadcasted_iota(jnp.int32, (count, count), 0) == lax.broadcasted_iota(jnp.int32, (count, count), 1)
        return jnp.sum(jnp.where(at, spread, jnp.zeros_like(spread)), axis=1, keepdims=True)

    oi_ref[...] = upright(occ_lanes[...], OT)
    vb_ref[...] = upright(virt_lanes[...], VT)
    for a in range(VL):
        ml_ref[:, a * OT : (a + 1) * OT] = occ_lanes[...] ^ virt_ref[row * VL + a]
    for a in range(VC):
        vl_ref[:, a * VT : (a + 1) * VT] = virt_lanes[...] ^ virt_ref[col * VC + a]

    def l_step(a, carry):
        rows = pl.ds(pl.multiple_of(a * VT, VT), VT)
        labels = vb_ref[...] ^ virt_ref[row * VL + a]
        lmask[rows, :] = jnp.where(labels == vl_ref[...], l_ref[rows, :], 0.0)
        return carry

    lax.fori_loop(0, VL, l_step, 0)
    lx[core, z, yme] = lmask[...].T

    for a in range(VL):
        row_s[:, a * VT : (a + 1) * VT] = ve_lanes[...] + ve_ref[row * VL + a]
    oe_up[...] = upright(oe_lanes[...], OT)
    load_t.wait()
    for h in range(2):
        high, low = split2(tt[h])
        part_s = dot_nt(p_ref[...], high) + dot_nt(p_ref[...], low)
        for i in range(OL // 2):
            to = (h * 3 + i) * OT
            s_ref[:, to : to + OT] = part_s[:, i * OT : (i + 1) * OT]
    pl.semaphore_wait(bar, 21)

    def peer(ref, index):
        return ref.at[pl.ds(pl.multiple_of(index * 32, 32), 32), :]

    def a2a_copy(d):
        return rc(peer(s_ref, col ^ d), peer(raw, col), A2A + d, (row, col ^ d))

    yt = rc(tt_ref.at[1 - yh], tx.at[x, yh], YT, opp)
    yt.start()
    x1 = [rc(tt_ref.at[yh], tx.at[x, yh], X1 + n, dev) for n, dev in enumerate((right, left))]
    for copy in x1:
        copy.start()
    lax.fori_loop(1, 16, lambda d, n: (a2a_copy(d).start(), n)[1], 0)
    own_t = pltpu.make_async_copy(tt_ref.at[yh], tx.at[x, yh], lsem.at[0])
    own_t.start()
    own_s = pltpu.make_async_copy(peer(s_ref, col), peer(raw, col), lsem.at[1])
    own_s.start()
    own_l = lx.at[core, z, yme]
    ydevs = [(row, ycol), (yrow, ycol), opp]
    yidx = [yh * 2 + 1 - yl, (1 - yh) * 2 + 1 - yl, (1 - yh) * 2 + yl]
    ly = [rc(own_l, own_l, LY + n, dev) for n, dev in enumerate(ydevs[:2])]
    ly[0].start()
    ly[1].start()
    lz = [rc(own_l, own_l, LZ + n, dev) for n, dev in enumerate((up, down))]
    for copy in lz:
        copy.start()

    order = [(xp, 1 - yh), (xm, 1 - yh), (xo, 1 - yh), (xo, yh), (xp, yh), (xm, yh), (x, 1 - yh), (x, yh)]

    def w_copy(t):
        dx, dy = order[t]
        return pltpu.make_async_copy(w_ref.at[dy * 4 + dx], wbuf.at[t % 2], wsem.at[t % 2])

    w_copy(0).start()
    w_copy(1).start()

    def w_split(t):
        dx, dy = order[t]
        own = ml_ref[...]

        def step(a, carry):
            rows = pl.ds(pl.multiple_of(a * OT, OT), OT)
            labels = oi_ref[...] ^ virt_ref[(dy * 4 + dx) * VL + a]
            kept = jnp.where(labels == own, wbuf[t % 2, rows, :], 0.0)
            high, low = split2(kept)
            w_hi[rows, :] = high
            w_lo[rows, :] = low
            return carry

        lax.fori_loop(0, VL, step, 0)

    def w_mm(t):
        def step(n, carry):
            rows = pl.ds(pl.multiple_of(n * 256, 256), 256)
            high, low = w_hi[rows, :], w_lo[rows, :]
            part[t, rows, :] = dot(high, ca_hi[...]) + dot(high, ca_lo[...]) + dot(low, ca_hi[...])
            return carry

        lax.fori_loop(0, CK // 256, step, 0)

    def cyc(t):
        if t > 0:
            w_copy(t).wait()
            w_split(t)
            if t + 2 < 8:
                w_copy(t + 2).start()
        w_mm(t)

    def add_into(dst, src):
        def step(n, carry):
            rows = pl.ds(pl.multiple_of(n * 96, 96), 96)
            dst[rows, :] = dst[rows, :] + src[rows, :]
            return carry

        lax.fori_loop(0, CK // 96, step, 0)

    w_copy(0).wait()
    w_split(0)
    w_copy(2).start()

    own_t.wait()
    yt.wait_send()
    pltpu.make_async_remote_copy(
        src_ref=tt_ref.at[1 - yh], dst_ref=tx.at[x, 1 - yh], send_sem=ssem.at[YT], recv_sem=rsem.at[YT],
        device_id=opp, device_id_type=MESH,
    ).wait_recv()
    x1b = [rc(tx.at[x, 1 - yh], tx.at[x, 1 - yh], X1 + 2 + n, dev) for n, dev in enumerate((right, left))]
    for copy in x1b:
        copy.start()

    x2 = []

    def pass_on(h, late):
        base = X1 + 2 * late
        rc(tx.at[xm, h], tx.at[xm, h], base, left).wait_recv()
        rc(tx.at[xp, h], tx.at[xp, h], base + 1, right).wait_recv()
        for n, (sx, rows, dev) in enumerate(((xm, upper, right), (xp, lower, left))):
            copy = rc(tx.at[sx, h, rows], tx.at[sx, h, rows], X2 + 2 * late + n, dev)
            copy.start()
            x2.append(copy)

    upper, lower = pl.ds(0, HIJ // 2), pl.ds(HIJ // 2, HIJ // 2)
    pass_on(yh, 0)

    lz2 = []

    def pass_block(n, src_y):
        rc(lx.at[core, zm, src_y], lx.at[core, zm, src_y], LZ + 2 * n, down).wait_recv()
        rc(lx.at[core, zp, src_y], lx.at[core, zp, src_y], LZ + 2 * n + 1, up).wait_recv()
        for m, (sz, first, dev) in enumerate(((zm, 0, up), (zp, CD // 2, down))):
            piece = lx.at[core, sz, src_y, pl.ds(first, CD // 2)]
            copy = rc(piece, piece, LZ2 + 2 * n + m, dev)
            copy.start()
            lz2.append(copy)

    pass_block(0, yme)

    own_s.wait()

    def a2a_wait(d, carry):
        a2a_copy(d).wait_send()
        rc(peer(s_ref, col), peer(raw, col ^ d), A2A + d, (row, col ^ d)).wait_recv()
        return carry

    lax.fori_loop(1, 16, a2a_wait, 0)

    def ca_step(c, carry):
        for i in range(OL):
            parts = [
                raw[pl.ds(pl.multiple_of(c * 32 + b * VL, VL), VL), i * OT : (i + 1) * OT] for b in range(VC)
            ]
            wide = jnp.concatenate(parts, axis=1)
            for n in range(3):
                ca[n, pl.ds(c * OL + i, VL, stride=OT), :] = wide[:, n * THIRD : (n + 1) * THIRD]
        return carry

    lax.fori_loop(0, 16, ca_step, 0)
    for n in range(3):
        high, low = split2(ca[n])
        ca_hi[:, n * THIRD : (n + 1) * THIRD] = high
        ca_lo[:, n * THIRD : (n + 1) * THIRD] = low

    lanes3 = [pl.ds(n * THIRD, THIRD) for n in range(3)]
    top, bottom = pl.ds(0, CK // 2), pl.ds(CK // 2, CK // 2)
    direct = [
        rc(part.at[0], recv.at[0], RS + 0, right),
        rc(part.at[1], recv.at[1], RS + 1, left),
        rc(part.at[2], recv.at[2], RS + 2, opp),
        rc(part.at[4, bottom], recv.at[4, bottom], RS + 3, right),
        rc(part.at[5, top], recv.at[5, top], RS + 4, left),
    ]
    first_hop = [
        [
            rc(part.at[3, rows, lanes], recv.at[3, rows, lanes], RS + 5 + 3 * m + n, dev)
            for m, (rows, dev) in enumerate(((top, right), (bottom, left)))
        ]
        for n, lanes in enumerate(lanes3)
    ]
    second_hop = [
        [
            rc(part.at[t, rows, lanes], recv.at[t, rows, lanes], RS + 11 + 3 * m + n, dev)
            for m, (t, rows, dev) in enumerate(((4, top, right), (5, bottom, left)))
        ]
        for n, lanes in enumerate(lanes3)
    ]
    mine, other = [pl.ds(pl.multiple_of(h * (CD // 2), CD // 2), CD // 2) for h in (yh, 1 - yh)]

    def over_z(n):
        block = lx.at[core, z, yidx[n]]
        if n < 2:
            rc(own_l, block, LY + n, ydevs[n]).wait_recv()
            piece = lx.at[core, z, yidx[n], mine]
            copy = rc(piece, piece, LY2 + n, ydevs[1 - n])
            copy.start()
            ly.append(copy)
        else:
            for m, rows in ((0, other), (1, mine)):
                piece = lx.at[core, z, yidx[n], rows]
                rc(piece, piece, LY2 + m, ydevs[1 - m]).wait_recv()
        for m, dev in enumerate((up, down)):
            copy = rc(block, block, LZ + 2 + 2 * n + m, dev)
            copy.start()
            lz.append(copy)

    cyc(0)
    direct[0].start()
    pass_on(1 - yh, 1)
    over_z(0)
    over_z(1)
    cyc(1)
    direct[1].start()
    cyc(2)
    direct[2].start()

    over_z(2)
    lc = [rc(lx.at[core, zz], lx.at[core, zz], LC + n, mate) for n, zz in enumerate((z, zm, zp, zo))]
    lc[0].start()

    cyc(3)
    cyc(4)
    direct[3].start()
    cyc(5)
    direct[4].start()
    pass_block(1, yidx[0])
    pass_block(2, yidx[1])
    cyc(6)
    cyc(7)

    direct[0].wait_recv()
    direct[1].wait_recv()
    yr = []
    for n, lanes in enumerate(lanes3):
        part[6, :, lanes] = part[6, :, lanes] + (recv[0, :, lanes] + recv[1, :, lanes])
        copy = rc(part.at[6, :, lanes], yrecv.at[:, lanes], YR + n, opp)
        copy.start()
        yr.append(copy)

    pass_block(3, yidx[2])
    lc[1].start()
    lc[2].start()

    direct[2].wait_recv()
    for n, lanes in enumerate(lanes3):
        part[3, :, lanes] = part[3, :, lanes] + recv[2, :, lanes]
        for copy in first_hop[n]:
            copy.start()

    def relay(n):
        lanes = lanes3[n]
        for m, (t, rows) in enumerate(((4, top), (5, bottom))):
            first_hop[n][m].wait_recv()
            part[t, rows, lanes] = part[t, rows, lanes] + recv[3, rows, lanes]
            second_hop[n][m].start()

    relay(0)
    relay(1)

    for n, src_y in enumerate([yme] + yidx):
        for m, (first, dev) in enumerate(((0, down), (CD // 2, up))):
            piece = lx.at[core, zo, src_y, pl.ds(first, CD // 2)]
            rc(piece, piece, LZ2 + 2 * n + m, dev).wait_recv()
    lc[3].start()

    for h in range(2):
        oacc[h] = jnp.zeros((HIJ, AB), F32)

    def ladder(sx, kc, sy):
        source = sy * 4 + sx
        zz, ylo = source // 2, source % 2
        lanes = pl.ds(pl.multiple_of(kc * CD, CD), CD)
        t_hi, t_lo = split2(tx[sx, sy, :, lanes])
        both = jnp.concatenate([t_hi, t_lo], axis=0)
        for h in range(2):
            high, low = split2(lx[kc, zz, h * 2 + ylo])
            wide = dot(both, high)
            oacc[h] = oacc[h] + (wide[:HIJ] + wide[HIJ:] + dot(t_hi, low))

    def ladder_run(kc):
        lax.fori_loop(0, 8, lambda n, carry: (ladder(n % 4, kc, n // 4), carry)[1], 0)

    def back_copy(n, d):
        return rc(
            cp.at[n, col ^ d], d3.at[n, col], BACK + 16 * n + d, (row, col ^ d)
        )

    own_d = [
        pltpu.make_async_copy(cp.at[n, col], d3.at[n, col], lsem.at[1 + n])
        for n, lanes in enumerate(lanes3)
    ]

    def finish(n):
        lanes = lanes3[n]
        for copy in second_hop[n] + [yr[n]]:
            copy.wait_recv()
        if n == 0:
            direct[3].wait_recv()
            direct[4].wait_recv()
        value = (part[7, :, lanes] + recv[4, :, lanes]) + (recv[5, :, lanes] + yrecv[:, lanes])
        high, low = split2(value)
        rest = (value - high.astype(F32) - low.astype(F32)).astype(BF16)
        sel = q_ref[...]
        cp[n] = (dot(sel, high) + dot(sel, low) + dot(sel, rest)).reshape(16, BLK, THIRD)
        lax.fori_loop(1, 16, lambda d, carry: (back_copy(n, d).start(), carry)[1], 0)
        own_d[n].start()

    for base, rows, dev in ((0, upper, left), (1, lower, right)):
        for h, late in ((yh, 0), (1 - yh, 1)):
            rc(tx.at[xo, h, rows], tx.at[xo, h, rows], X2 + 2 * late + base, dev).wait_recv()
    relay(2)
    ladder_run(core)
    finish(0)
    finish(1)
    finish(2)
    for n, zz in enumerate((z, zm, zp, zo)):
        rc(lx.at[1 - core, zz], lx.at[1 - core, zz], LC + n, mate).wait_recv()
    ladder_run(1 - core)
    bands = [pl.ds(n * OT, OT) for n in range(OL // 2)]
    ob = [
        rc(oacc.at[1 - yh, rows], lad.at[yh, rows], k, opp) for rows, k in zip(bands, (OB, LY + 2, BACK))
    ]
    for copy in ob:
        copy.start()

    inverse = tx.at[xo]
    for h in range(2):
        for n, rows in enumerate(bands):
            inverse[h, rows, :] = 1.0 / (row_s[...] - (oe_up[...] + oe_ref[col * OL + h * 3 + n]))

    def unpack(c):
        wide = [
            jnp.concatenate([d3[n, c, pl.ds(i, VL, stride=OL), :] for n in range(3)], axis=1) for i in range(OL)
        ]
        for b in range(VC):
            rows = pl.ds(pl.multiple_of(c * 32 + b * VL, VL), VL)
            raw[rows, :] = jnp.concatenate([value[:, b * OT : (b + 1) * OT] for value in wide], axis=1)

    def back_wait(d):
        for n in range(3):
            leaving = back_copy(n, d)
            leaving.wait_send()
            arriving = rc(cp.at[n, col], d3.at[n, col ^ d], BACK + 16 * n + d, (row, col ^ d))
            arriving.wait_recv()
        unpack(col ^ d)

    def gather_rows(ref, group):
        starts = [pl.multiple_of(zz * 128 + group * 64, 64) for zz in range(4)]
        return jnp.concatenate([ref[pl.ds(start, 64), :] for start in starts], axis=0)

    def turn(group):
        xt = gather_rows(raw, group).T
        turned[0] = xt[:HIJ]
        turned[1] = xt[HIJ:]
        return gather_rows(p_ref, group)

    def selected(value, sel):
        high, low = split2(value)
        rest = (value - high.astype(F32) - low.astype(F32)).astype(BF16)
        return dot(high, sel) + dot(low, sel) + dot(rest, sel)

    for n in range(3):
        own_d[n].wait()
    unpack(col)
    lax.fori_loop(1, 8, lambda k, carry: (back_wait((k // 2) * 4 + k % 2), carry)[1], 0)
    sel = turn(yl)
    for i in range(OL):
        h, rows = i // 3, pl.ds((i % 3) * OT, OT)
        tt[h, rows, :] = selected(turned[h, rows, :], sel)
    lax.fori_loop(0, 8, lambda k, carry: (back_wait((k // 2) * 4 + 2 + k % 2), carry)[1], 0)
    sel = turn(1 - yl)
    for i in range(OL):
        h, rows = i // 3, pl.ds((i % 3) * OT, OT)
        tt[h, rows, :] = (tt[h, rows, :] + selected(turned[h, rows, :], sel)) * inverse[h, rows, :]
    def write(h, n):
        place = pl.ds(pl.multiple_of(h * HIJ + n * OT, OT), OT)
        return pltpu.make_async_copy(tt.at[h, bands[n]], out_ref.at[place], osem.at[h, n])

    for n, rows in enumerate(bands):
        tt[yh, rows, :] = oacc[yh, rows, :] * inverse[yh, rows, :] + tt[yh, rows, :]
        write(yh, n).start()

    for copy in x1 + x1b + x2 + ly + lz + lz2 + lc + direct + sum(first_hop + second_hop, []) + yr:
        copy.wait_send()
    for n, rows in enumerate(bands):
        other_half = lad.at[1 - yh, rows]
        rc(oacc.at[yh, rows], other_half, (OB, LY + 2, BACK)[n], opp).wait_recv()
        tt[1 - yh, rows, :] = lad[1 - yh, rows, :] * inverse[1 - yh, rows, :] + tt[1 - yh, rows, :]
        write(1 - yh, n).start()
    for copy in ob:
        copy.wait_send()
    for n in range(OL // 2):
        write(yh, n).wait()
        write(1 - yh, n).wait()


def to_peers():
    c, b, a = np.meshgrid(np.arange(16), np.arange(VC), np.arange(VL), indexing="ij")
    table = np.zeros((AB, AB), np.float32)
    table[(c * 32 + b * VL + a).reshape(-1), (a * VT + c * VC + b).reshape(-1)] = 1.0
    return table


def from_cycle():
    a, c, i = np.meshgrid(np.arange(VL), np.arange(16), np.arange(OL), indexing="ij")
    table = np.zeros((CK, CK), np.float32)
    table[(c * BLK + a * OL + i).reshape(-1), (a * OT + c * OL + i).reshape(-1)] = 1.0
    return table


def body(amps, ladder_ints, cycle_ints, virt_irrep, occ_irrep, virt_energy, occ_energy):
    turned = amps.T.reshape(2, HIJ, AB)
    anywhere = pl.BlockSpec(memory_space=pl.ANY)
    vmem = pl.BlockSpec(memory_space=pltpu.VMEM)
    smem = pl.BlockSpec(memory_space=pltpu.SMEM)
    update = pl.pallas_call(
        kernel,
        out_shape=jax.ShapeDtypeStruct((OL * OT, AB), F32),
        in_specs=[smem] * 3 + [anywhere, vmem, anywhere] + [vmem] * 6,
        out_specs=anywhere,
        scratch_shapes=[
            pltpu.VMEM((1, AB), F32),
            pltpu.VMEM((OT, 1), F32),
            pltpu.VMEM((2, HIJ, AB), F32),
            pltpu.VMEM((2, HIJ, AB // 2), F32),
            pltpu.VMEM((2, HIJ, AB), F32),
            pltpu.VMEM((AB, OL * OT), F32),
            pltpu.VMEM((4, 2, HIJ, AB), F32),
            pltpu.VMEM((2, 4, 4, CD, AB), F32),
            pltpu.VMEM((AB, OL * OT), F32),
            pltpu.VMEM((3, CK, THIRD), F32),
            pltpu.VMEM((CK, BJ), BF16),
            pltpu.VMEM((CK, BJ), BF16),
            pltpu.VMEM((2, CK, CK), F32),
            pltpu.VMEM((CK, CK), BF16),
            pltpu.VMEM((CK, CK), BF16),
            pltpu.VMEM((8, CK, BJ), F32),
            pltpu.VMEM((6, CK, BJ), F32),
            pltpu.VMEM((CK, BJ), F32),
            pltpu.VMEM((2, HIJ, AB), F32),
            pltpu.VMEM((AB, CD), F32),
            pltpu.VMEM((3, 16, BLK, THIRD), F32),
            pltpu.VMEM((3, 16, BLK, THIRD), F32),
            pltpu.VMEM((1, CK), jnp.int32),
            pltpu.VMEM((1, CD), jnp.int32),
            pltpu.VMEM((OT, 1), jnp.int32),
            pltpu.VMEM((VT, 1), jnp.int32),
            pltpu.SemaphoreType.DMA((NSEM,)),
            pltpu.SemaphoreType.DMA((NSEM,)),
            pltpu.SemaphoreType.DMA((2,)),
            pltpu.SemaphoreType.DMA((6,)),
            pltpu.SemaphoreType.DMA((2, 3)),
        ],
        compiler_params=pltpu.CompilerParams(
            collective_id=0, has_side_effects=True, vmem_limit_bytes=67043328
        ),
    )(
        virt_irrep, virt_energy, occ_energy, turned, ladder_ints, cycle_ints.reshape(8, CK, CK),
        virt_irrep.reshape(1, VT), occ_irrep.reshape(1, OT), virt_energy.reshape(1, VT), occ_energy.reshape(1, OT),
        jnp.asarray(to_peers(), BF16), jnp.asarray(from_cycle(), BF16),
    )
    return update.T


def solution(mesh):
    placed = (P("row", "col"), P("row", "col"), P(None, "row"), P(), P(), P(), P())
    return jax.shard_map(
        body, mesh=mesh, in_specs=placed, out_specs=P("row", "col"), check_vma=False
    )
```

```python
import functools

import jax
import jax.numpy as jnp
import numpy as np
from jax import lax
from jax.experimental import pallas as pl
from jax.experimental.pallas import tpu as pltpu
from jax.sharding import PartitionSpec as P

MESH = pl.DeviceIdType.MESH
F32, BF16 = jnp.float32, jnp.bfloat16

VT, OT = 64, 96
VL, OL, VC = 8, 6, 4
CK = VL * OT
BJ = VC * OT
BLK = VL * OL
THIRD = BJ // 3
AB = VL * VT
CD = 256
HIJ = OL * OT // 2

A2A, BACK, YT, X1, X2, LY = 0, 16, 64, 65, 69, 73
LZ, LZ2, LC, OB, RS, YR, LY2 = 76, 84, 92, 96, 97, 114, 117
NSEM = 119


def split2(value):
    high = value.astype(BF16)
    low = (value - high.astype(F32)).astype(BF16)
    return high, low


def dot_nt(a, b):
    return lax.dot_general(a, b, (((1,), (1,)), ((), ())), preferred_element_type=F32)


def dot(a, b):
    return jnp.dot(a, b, preferred_element_type=F32)


def kernel(
    virt_ref, ve_ref, oe_ref, tt_ref, l_ref, w_ref, virt_lanes, occ_lanes, ve_lanes, oe_lanes, p_ref, q_ref,
    out_ref,
    row_s, oe_up, lad, turned, tt, s_ref, tx, lx, raw, ca, ca_hi, ca_lo, wbuf, w_hi, w_lo, part, recv, yrecv, oacc, lmask, cp, d3, ml_ref, vl_ref, oi_ref, vb_ref,
    ssem, rsem, wsem, lsem, osem,
):
    row, col = lax.axis_index("row"), lax.axis_index("col")
    yh, x = row // 4, row % 4
    z, yl, core = col // 4, (col // 2) % 2, col % 2
    yme = yh * 2 + yl
    xp, xm, xo = (x + 1) % 4, (x + 3) % 4, (x + 2) % 4
    zp, zm, zo = (z + 1) % 4, (z + 3) % 4, (z + 2) % 4
    right, left = (yh * 4 + xp, col), (yh * 4 + xm, col)
    up, down = (row, zp * 4 + col % 4), (row, zm * 4 + col % 4)
    yrow = (1 - yh) * 4 + x
    ycol = z * 4 + (1 - yl) * 2 + core
    opp = (yrow, col)
    mate = (row, z * 4 + yl * 2 + (1 - core))

    def rc(src, dst, k, dev):
        return pltpu.make_async_remote_copy(
            src_ref=src, dst_ref=dst, send_sem=ssem.at[k], recv_sem=rsem.at[k],
            device_id=dev, device_id_type=MESH,
        )

    bar = pltpu.get_barrier_semaphore()

    def greet(d, carry):
        pl.semaphore_signal(bar, inc=1, device_id=(row, col ^ d), device_id_type=MESH)
        return carry

    lax.fori_loop(1, 16, greet, 0)
    for dev in (right, left, up, down, opp, (yrow, ycol)):
        pl.semaphore_signal(bar, inc=1, device_id=dev, device_id_type=MESH)

    load_t = pltpu.make_async_copy(tt_ref, tt, lsem.at[0])
    load_t.start()

    def upright(lanes, count):
        spread = jnp.broadcast_to(lanes, (count, count))
        at = lax.broadcasted_iota(jnp.int32, (count, count), 0) == lax.broadcasted_iota(jnp.int32, (count, count), 1)
        return jnp.sum(jnp.where(at, spread, jnp.zeros_like(spread)), axis=1, keepdims=True)

    oi_ref[...] = upright(occ_lanes[...], OT)
    vb_ref[...] = upright(virt_lanes[...], VT)
    for a in range(VL):
        ml_ref[:, a * OT : (a + 1) * OT] = occ_lanes[...] ^ virt_ref[row * VL + a]
    for a in range(VC):
        vl_ref[:, a * VT : (a + 1) * VT] = virt_lanes[...] ^ virt_ref[col * VC + a]

    def l_step(a, carry):
        rows = pl.ds(pl.multiple_of(a * VT, VT), VT)
        labels = vb_ref[...] ^ virt_ref[row * VL + a]
        lmask[rows, :] = jnp.where(labels == vl_ref[...], l_ref[rows, :], 0.0)
        return carry

    lax.fori_loop(0, VL, l_step, 0)
    lx[core, z, yme] = lmask[...].T

    for a in range(VL):
        row_s[:, a * VT : (a + 1) * VT] = ve_lanes[...] + ve_ref[row * VL + a]
    oe_up[...] = upright(oe_lanes[...], OT)
    load_t.wait()
    for h in range(2):
        high, low = split2(tt[h])
        part_s = dot_nt(p_ref[...], high) + dot_nt(p_ref[...], low)
        for i in range(OL // 2):
            to = (h * 3 + i) * OT
            s_ref[:, to : to + OT] = part_s[:, i * OT : (i + 1) * OT]
    pl.semaphore_wait(bar, 21)

    def peer(ref, index):
        return ref.at[pl.ds(pl.multiple_of(index * 32, 32), 32), :]

    def a2a_copy(d):
        return rc(peer(s_ref, col ^ d), peer(raw, col), A2A + d, (row, col ^ d))

    yt = rc(tt_ref.at[1 - yh], tx.at[x, yh], YT, opp)
    yt.start()
    x1 = [rc(tt_ref.at[yh], tx.at[x, yh], X1 + n, dev) for n, dev in enumerate((right, left))]
    for copy in x1:
        copy.start()
    lax.fori_loop(1, 16, lambda d, n: (a2a_copy(d).start(), n)[1], 0)
    own_t = pltpu.make_async_copy(tt_ref.at[yh], tx.at[x, yh], lsem.at[0])
    own_t.start()
    own_s = pltpu.make_async_copy(peer(s_ref, col), peer(raw, col), lsem.at[1])
    own_s.start()
    own_l = lx.at[core, z, yme]
    ydevs = [(row, ycol), (yrow, ycol), opp]
    yidx = [yh * 2 + 1 - yl, (1 - yh) * 2 + 1 - yl, (1 - yh) * 2 + yl]
    ly = [rc(own_l, own_l, LY + n, dev) for n, dev in enumerate(ydevs[:2])]
    ly[0].start()
    ly[1].start()
    lz = [rc(own_l, own_l, LZ + n, dev) for n, dev in enumerate((up, down))]
    for copy in lz:
        copy.start()

    order = [(xp, 1 - yh), (xm, 1 - yh), (xo, 1 - yh), (xo, yh), (xp, yh), (xm, yh), (x, 1 - yh), (x, yh)]

    def w_copy(t):
        dx, dy = order[t]
        return pltpu.make_async_copy(w_ref.at[dy * 4 + dx], wbuf.at[t % 2], wsem.at[t % 2])

    w_copy(0).start()
    w_copy(1).start()

    def w_split(t):
        dx, dy = order[t]
        own = ml_ref[...]

        def step(a, carry):
            rows = pl.ds(pl.multiple_of(a * OT, OT), OT)
            labels = oi_ref[...] ^ virt_ref[(dy * 4 + dx) * VL + a]
            kept = jnp.where(labels == own, wbuf[t % 2, rows, :], 0.0)
            high, low = split2(kept)
            w_hi[rows, :] = high
            w_lo[rows, :] = low
            return carry

        lax.fori_loop(0, VL, step, 0)

    def w_mm(t):
        def step(n, carry):
            rows = pl.ds(pl.multiple_of(n * 256, 256), 256)
            high, low = w_hi[rows, :], w_lo[rows, :]
            part[t, rows, :] = dot(high, ca_hi[...]) + dot(high, ca_lo[...]) + dot(low, ca_hi[...])
            return carry

        lax.fori_loop(0, CK // 256, step, 0)

    def cyc(t):
        if t > 0:
            w_copy(t).wait()
            w_split(t)
            if t + 2 < 8:
                w_copy(t + 2).start()
        w_mm(t)

    def add_into(dst, src):
        def step(n, carry):
            rows = pl.ds(pl.multiple_of(n * 96, 96), 96)
            dst[rows, :] = dst[rows, :] + src[rows, :]
            return carry

        lax.fori_loop(0, CK // 96, step, 0)

    w_copy(0).wait()
    w_split(0)
    w_copy(2).start()

    own_t.wait()
    yt.wait_send()
    pltpu.make_async_remote_copy(
        src_ref=tt_ref.at[1 - yh], dst_ref=tx.at[x, 1 - yh], send_sem=ssem.at[YT], recv_sem=rsem.at[YT],
        device_id=opp, device_id_type=MESH,
    ).wait_recv()
    x1b = [rc(tx.at[x, 1 - yh], tx.at[x, 1 - yh], X1 + 2 + n, dev) for n, dev in enumerate((right, left))]
    for copy in x1b:
        copy.start()

    x2 = []

    def pass_on(h, late):
        base = X1 + 2 * late
        rc(tx.at[xm, h], tx.at[xm, h], base, left).wait_recv()
        rc(tx.at[xp, h], tx.at[xp, h], base + 1, right).wait_recv()
        for n, (sx, rows, dev) in enumerate(((xm, upper, right), (xp, lower, left))):
            copy = rc(tx.at[sx, h, rows], tx.at[sx, h, rows], X2 + 2 * late + n, dev)
            copy.start()
            x2.append(copy)

    upper, lower = pl.ds(0, HIJ // 2), pl.ds(HIJ // 2, HIJ // 2)
    pass_on(yh, 0)

    lz2 = []

    def pass_block(n, src_y):
        rc(lx.at[core, zm, src_y], lx.at[core, zm, src_y], LZ + 2 * n, down).wait_recv()
        rc(lx.at[core, zp, src_y], lx.at[core, zp, src_y], LZ + 2 * n + 1, up).wait_recv()
        for m, (sz, first, dev) in enumerate(((zm, 0, up), (zp, CD // 2, down))):
            piece = lx.at[core, sz, src_y, pl.ds(first, CD // 2)]
            copy = rc(piece, piece, LZ2 + 2 * n + m, dev)
            copy.start()
            lz2.append(copy)

    pass_block(0, yme)

    own_s.wait()

    def a2a_wait(d, carry):
        a2a_copy(d).wait_send()
        rc(peer(s_ref, col), peer(raw, col ^ d), A2A + d, (row, col ^ d)).wait_recv()
        return carry

    lax.fori_loop(1, 16, a2a_wait, 0)

    def ca_step(c, carry):
        for i in range(OL):
            parts = [
                raw[pl.ds(pl.multiple_of(c * 32 + b * VL, VL), VL), i * OT : (i + 1) * OT] for b in range(VC)
            ]
            wide = jnp.concatenate(parts, axis=1)
            for n in range(3):
                ca[n, pl.ds(c * OL + i, VL, stride=OT), :] = wide[:, n * THIRD : (n + 1) * THIRD]
        return carry

    lax.fori_loop(0, 16, ca_step, 0)
    for n in range(3):
        high, low = split2(ca[n])
        ca_hi[:, n * THIRD : (n + 1) * THIRD] = high
        ca_lo[:, n * THIRD : (n + 1) * THIRD] = low

    lanes3 = [pl.ds(n * THIRD, THIRD) for n in range(3)]
    top, bottom = pl.ds(0, CK // 2), pl.ds(CK // 2, CK // 2)
    direct = [
        rc(part.at[0], recv.at[0], RS + 0, right),
        rc(part.at[1], recv.at[1], RS + 1, left),
        rc(part.at[2], recv.at[2], RS + 2, opp),
        rc(part.at[4, bottom], recv.at[4, bottom], RS + 3, right),
        rc(part.at[5, top], recv.at[5, top], RS + 4, left),
    ]
    first_hop = [
        [
            rc(part.at[3, rows, lanes], recv.at[3, rows, lanes], RS + 5 + 3 * m + n, dev)
            for m, (rows, dev) in enumerate(((top, right), (bottom, left)))
        ]
        for n, lanes in enumerate(lanes3)
    ]
    second_hop = [
        [
            rc(part.at[t, rows, lanes], recv.at[t, rows, lanes], RS + 11 + 3 * m + n, dev)
            for m, (t, rows, dev) in enumerate(((4, top, right), (5, bottom, left)))
        ]
        for n, lanes in enumerate(lanes3)
    ]
    mine, other = [pl.ds(pl.multiple_of(h * (CD // 2), CD // 2), CD // 2) for h in (yh, 1 - yh)]

    def over_z(n):
        block = lx.at[core, z, yidx[n]]
        if n < 2:
            rc(own_l, block, LY + n, ydevs[n]).wait_recv()
            piece = lx.at[core, z, yidx[n], mine]
            copy = rc(piece, piece, LY2 + n, ydevs[1 - n])
            copy.start()
            ly.append(copy)
        else:
            for m, rows in ((0, other), (1, mine)):
                piece = lx.at[core, z, yidx[n], rows]
                rc(piece, piece, LY2 + m, ydevs[1 - m]).wait_recv()
        for m, dev in enumerate((up, down)):
            copy = rc(block, block, LZ + 2 + 2 * n + m, dev)
            copy.start()
            lz.append(copy)

    cyc(0)
    direct[0].start()
    pass_on(1 - yh, 1)
    cyc(1)
    direct[1].start()
    over_z(0)
    over_z(1)
    cyc(2)
    direct[2].start()

    over_z(2)
    lc = [rc(lx.at[core, zz], lx.at[core, zz], LC + n, mate) for n, zz in enumerate((z, zm, zp, zo))]
    lc[0].start()

    cyc(3)
    cyc(4)
    direct[3].start()
    cyc(5)
    direct[4].start()
    pass_block(1, yidx[0])
    pass_block(2, yidx[1])
    cyc(6)
    cyc(7)

    direct[0].wait_recv()
    direct[1].wait_recv()
    yr = []
    for n, lanes in enumerate(lanes3):
        part[6, :, lanes] = part[6, :, lanes] + (recv[0, :, lanes] + recv[1, :, lanes])
        copy = rc(part.at[6, :, lanes], yrecv.at[:, lanes], YR + n, opp)
        copy.start()
        yr.append(copy)

    pass_block(3, yidx[2])
    lc[1].start()
    lc[2].start()

    direct[2].wait_recv()
    for n, lanes in enumerate(lanes3):
        part[3, :, lanes] = part[3, :, lanes] + recv[2, :, lanes]
        for copy in first_hop[n]:
            copy.start()

    def relay(n):
        lanes = lanes3[n]
        for m, (t, rows) in enumerate(((4, top), (5, bottom))):
            first_hop[n][m].wait_recv()
            part[t, rows, lanes] = part[t, rows, lanes] + recv[3, rows, lanes]
            second_hop[n][m].start()

    relay(0)
    relay(1)

    for n, src_y in enumerate([yme] + yidx):
        for m, (first, dev) in enumerate(((0, down), (CD // 2, up))):
            piece = lx.at[core, zo, src_y, pl.ds(first, CD // 2)]
            rc(piece, piece, LZ2 + 2 * n + m, dev).wait_recv()
    lc[3].start()

    for h in range(2):
        oacc[h] = jnp.zeros((HIJ, AB), F32)

    def ladder(sx, kc, sy):
        source = sy * 4 + sx
        zz, ylo = source // 2, source % 2
        lanes = pl.ds(pl.multiple_of(kc * CD, CD), CD)
        t_hi, t_lo = split2(tx[sx, sy, :, lanes])
        both = jnp.concatenate([t_hi, t_lo], axis=0)
        for h in range(2):
            high, low = split2(lx[kc, zz, h * 2 + ylo])
            wide = dot(both, high)
            oacc[h] = oacc[h] + (wide[:HIJ] + wide[HIJ:] + dot(t_hi, low))

    def ladder_run(kc):
        lax.fori_loop(0, 8, lambda n, carry: (ladder(n % 4, kc, n // 4), carry)[1], 0)

    def back_copy(n, d):
        return rc(
            cp.at[n, col ^ d], d3.at[n, col], BACK + 16 * n + d, (row, col ^ d)
        )

    own_d = [
        pltpu.make_async_copy(cp.at[n, col], d3.at[n, col], lsem.at[1 + n])
        for n, lanes in enumerate(lanes3)
    ]

    def finish(n):
        lanes = lanes3[n]
        for copy in second_hop[n] + [yr[n]]:
            copy.wait_recv()
        if n == 0:
            direct[3].wait_recv()
            direct[4].wait_recv()
        value = (part[7, :, lanes] + recv[4, :, lanes]) + (recv[5, :, lanes] + yrecv[:, lanes])
        high, low = split2(value)
        rest = (value - high.astype(F32) - low.astype(F32)).astype(BF16)
        sel = q_ref[...]
        cp[n] = (dot(sel, high) + dot(sel, low) + dot(sel, rest)).reshape(16, BLK, THIRD)
        lax.fori_loop(1, 16, lambda d, carry: (back_copy(n, d).start(), carry)[1], 0)
        own_d[n].start()

    for base, rows, dev in ((0, upper, left), (1, lower, right)):
        for h, late in ((yh, 0), (1 - yh, 1)):
            rc(tx.at[xo, h, rows], tx.at[xo, h, rows], X2 + 2 * late + base, dev).wait_recv()
    relay(2)
    ladder_run(core)
    finish(0)
    finish(1)
    finish(2)
    for n, zz in enumerate((z, zm, zp, zo)):
        rc(lx.at[1 - core, zz], lx.at[1 - core, zz], LC + n, mate).wait_recv()
    ladder_run(1 - core)
    bands = [pl.ds(n * OT, OT) for n in range(OL // 2)]
    ob = [
        rc(oacc.at[1 - yh, rows], lad.at[yh, rows], k, opp) for rows, k in zip(bands, (OB, LY + 2, BACK))
    ]
    for copy in ob:
        copy.start()

    inverse = tx.at[xo]
    for h in range(2):
        for n, rows in enumerate(bands):
            inverse[h, rows, :] = 1.0 / (row_s[...] - (oe_up[...] + oe_ref[col * OL + h * 3 + n]))

    def unpack(c):
        wide = [
            jnp.concatenate([d3[n, c, pl.ds(i, VL, stride=OL), :] for n in range(3)], axis=1) for i in range(OL)
        ]
        for b in range(VC):
            rows = pl.ds(pl.multiple_of(c * 32 + b * VL, VL), VL)
            raw[rows, :] = jnp.concatenate([value[:, b * OT : (b + 1) * OT] for value in wide], axis=1)

    def back_wait(d):
        for n in range(3):
            leaving = back_copy(n, d)
            leaving.wait_send()
            arriving = rc(cp.at[n, col], d3.at[n, col ^ d], BACK + 16 * n + d, (row, col ^ d))
            arriving.wait_recv()
        unpack(col ^ d)

    def gather_rows(ref, group):
        starts = [pl.multiple_of(zz * 128 + group * 64, 64) for zz in range(4)]
        return jnp.concatenate([ref[pl.ds(start, 64), :] for start in starts], axis=0)

    def turn(group):
        xt = gather_rows(raw, group).T
        turned[0] = xt[:HIJ]
        turned[1] = xt[HIJ:]
        return gather_rows(p_ref, group)

    def selected(value, sel):
        high, low = split2(value)
        rest = (value - high.astype(F32) - low.astype(F32)).astype(BF16)
        return dot(high, sel) + dot(low, sel) + dot(rest, sel)

    for n in range(3):
        own_d[n].wait()
    unpack(col)
    lax.fori_loop(1, 8, lambda k, carry: (back_wait((k // 2) * 4 + k % 2), carry)[1], 0)
    sel = turn(yl)
    for i in range(OL):
        h, rows = i // 3, pl.ds((i % 3) * OT, OT)
        tt[h, rows, :] = selected(turned[h, rows, :], sel)
    lax.fori_loop(0, 8, lambda k, carry: (back_wait((k // 2) * 4 + 2 + k % 2), carry)[1], 0)
    sel = turn(1 - yl)
    for i in range(OL):
        h, rows = i // 3, pl.ds((i % 3) * OT, OT)
        tt[h, rows, :] = (tt[h, rows, :] + selected(turned[h, rows, :], sel)) * inverse[h, rows, :]
    def write(h, n):
        place = pl.ds(pl.multiple_of(h * HIJ + n * OT, OT), OT)
        return pltpu.make_async_copy(tt.at[h, bands[n]], out_ref.at[place], osem.at[h, n])

    for n, rows in enumerate(bands):
        tt[yh, rows, :] = oacc[yh, rows, :] * inverse[yh, rows, :] + tt[yh, rows, :]
        write(yh, n).start()

    for copy in x1 + x1b + x2 + ly + lz + lz2 + lc + direct + sum(first_hop + second_hop, []) + yr:
        copy.wait_send()
    for n, rows in enumerate(bands):
        other_half = lad.at[1 - yh, rows]
        rc(oacc.at[yh, rows], other_half, (OB, LY + 2, BACK)[n], opp).wait_recv()
        tt[1 - yh, rows, :] = lad[1 - yh, rows, :] * inverse[1 - yh, rows, :] + tt[1 - yh, rows, :]
        write(1 - yh, n).start()
    for copy in ob:
        copy.wait_send()
    for n in range(OL // 2):
        write(yh, n).wait()
        write(1 - yh, n).wait()


def to_peers():
    c, b, a = np.meshgrid(np.arange(16), np.arange(VC), np.arange(VL), indexing="ij")
    table = np.zeros((AB, AB), np.float32)
    table[(c * 32 + b * VL + a).reshape(-1), (a * VT + c * VC + b).reshape(-1)] = 1.0
    return table


def from_cycle():
    a, c, i = np.meshgrid(np.arange(VL), np.arange(16), np.arange(OL), indexing="ij")
    table = np.zeros((CK, CK), np.float32)
    table[(c * BLK + a * OL + i).reshape(-1), (a * OT + c * OL + i).reshape(-1)] = 1.0
    return table


def body(amps, ladder_ints, cycle_ints, virt_irrep, occ_irrep, virt_energy, occ_energy):
    turned = amps.T.reshape(2, HIJ, AB)
    anywhere = pl.BlockSpec(memory_space=pl.ANY)
    vmem = pl.BlockSpec(memory_space=pltpu.VMEM)
    smem = pl.BlockSpec(memory_space=pltpu.SMEM)
    update = pl.pallas_call(
        kernel,
        out_shape=jax.ShapeDtypeStruct((OL * OT, AB), F32),
        in_specs=[smem] * 3 + [anywhere, vmem, anywhere] + [vmem] * 6,
        out_specs=anywhere,
        scratch_shapes=[
            pltpu.VMEM((1, AB), F32),
            pltpu.VMEM((OT, 1), F32),
            pltpu.VMEM((2, HIJ, AB), F32),
            pltpu.VMEM((2, HIJ, AB // 2), F32),
            pltpu.VMEM((2, HIJ, AB), F32),
            pltpu.VMEM((AB, OL * OT), F32),
            pltpu.VMEM((4, 2, HIJ, AB), F32),
            pltpu.VMEM((2, 4, 4, CD, AB), F32),
            pltpu.VMEM((AB, OL * OT), F32),
            pltpu.VMEM((3, CK, THIRD), F32),
            pltpu.VMEM((CK, BJ), BF16),
            pltpu.VMEM((CK, BJ), BF16),
            pltpu.VMEM((2, CK, CK), F32),
            pltpu.VMEM((CK, CK), BF16),
            pltpu.VMEM((CK, CK), BF16),
            pltpu.VMEM((8, CK, BJ), F32),
            pltpu.VMEM((6, CK, BJ), F32),
            pltpu.VMEM((CK, BJ), F32),
            pltpu.VMEM((2, HIJ, AB), F32),
            pltpu.VMEM((AB, CD), F32),
            pltpu.VMEM((3, 16, BLK, THIRD), F32),
            pltpu.VMEM((3, 16, BLK, THIRD), F32),
            pltpu.VMEM((1, CK), jnp.int32),
            pltpu.VMEM((1, CD), jnp.int32),
            pltpu.VMEM((OT, 1), jnp.int32),
            pltpu.VMEM((VT, 1), jnp.int32),
            pltpu.SemaphoreType.DMA((NSEM,)),
            pltpu.SemaphoreType.DMA((NSEM,)),
            pltpu.SemaphoreType.DMA((2,)),
            pltpu.SemaphoreType.DMA((6,)),
            pltpu.SemaphoreType.DMA((2, 3)),
        ],
        compiler_params=pltpu.CompilerParams(
            collective_id=0, has_side_effects=True, vmem_limit_bytes=67043328
        ),
    )(
        virt_irrep, virt_energy, occ_energy, turned, ladder_ints, cycle_ints.reshape(8, CK, CK),
        virt_irrep.reshape(1, VT), occ_irrep.reshape(1, OT), virt_energy.reshape(1, VT), occ_energy.reshape(1, OT),
        jnp.asarray(to_peers(), BF16), jnp.asarray(from_cycle(), BF16),
    )
    return update.T


def solution(mesh):
    placed = (P("row", "col"), P("row", "col"), P(None, "row"), P(), P(), P(), P())
    return jax.shard_map(
        body, mesh=mesh, in_specs=placed, out_specs=P("row", "col"), check_vma=False
    )
```
